32 devices in a mesh: seq: 8 (over z, x), head: 4 (over y, core).
Axes of the slice: x: 2, y: 2, z: 4, core: 2. Of those that a mesh axis runs over, the one named last changes fastest.
Arguments:
- queries: bfloat16 [2048, 4096], P('seq', 'head'), may hold values from -100 to 100
- keys_values: bfloat16 [2048, 2, 512], P('seq', None, 'head'), may hold values from -4.5 to 4.5
- cache_kv: bfloat16 [2048, 2, 512], P('seq', None, 'head'), may hold values from -4 to 4
- vertical_pages: int32 [4, 4], P('head'), may hold values from 0 to 15, as said below
- slash_shift: int32 [4, 3], P('head'), may hold values from 1 to 8, as said below
- slash_live: int32 [8, 4, 3], P('seq', 'head'), may hold values 0 or 1
- out_proj: bfloat16 [4096, 2048], P('head'), may hold values from -0.09375 to 0.09375
Outputs:
- projected: bfloat16 [2048, 2048], P('seq', 'head')
The draws below stay inside these ranges and needn't reach their ends.
Inputs may be any that keep to these rules, and one draw needn't show every extreme that they name: `vertical_pages`: each head group lists 4 distinct pages. `slash_shift`: each head group lists 3 distinct distances.
All inputs are finite; a program needn't handle non-finite values. No bound on the sum of `slash_live` on one device may be relied on, other than what follows from the above.
Results may differ from the reference program's by a relative error of at most 0.0057.
Values may be sent and summed in bfloat16 or wider, within the bound.
No kernel may reach another device: no remote copies, remote signals or barrier semaphores. Data moves between devices by JAX's collectives and lax.ppermute only.
A program may use at most 64 MiB of HBM per device.

```python
import jax
import jax.numpy as jnp
from jax import lax

D = 2048
HEADS = 32
KVH = 4
HD = 128
ROWS = 256
PAGE = 128
VPAGES = 4
SLASH = 3
SHARDS = 8
TOKENS = 2048
PPS = 2
CPAGES = 16


def joint_draw(key):
    query_key = jax.random.fold_in(key, 11)
    pair_key = jax.random.fold_in(key, 12)
    pair_store = jnp.clip(jax.random.normal(pair_key, (TOKENS, 2, KVH * HD), jnp.float32), -4.0, 4.0)
    query_store = jnp.clip(jax.random.normal(query_key, (TOKENS, HEADS * HD), jnp.float32), -4.0, 4.0)
    return (query_store, pair_store)


def draw_queries(key, part):
    return joint_draw(key)[0].astype(jnp.bfloat16)


def draw_keys_values(key, part):
    return joint_draw(key)[1].astype(jnp.bfloat16)


def draw_vertical_pages(key, part):
    group_keys = jax.random.split(jax.random.fold_in(key, 21), KVH)
    chosen = jax.vmap(lambda group_key: jax.random.permutation(group_key, CPAGES)[:VPAGES])(group_keys)
    return chosen.astype(jnp.int32)


def draw_slash_shift(key, part):
    group_keys = jax.random.split(jax.random.fold_in(key, 31), KVH)
    chosen = jax.vmap(lambda group_key: jax.random.permutation(group_key, SHARDS)[:SLASH] + 1)(group_keys)
    return chosen.astype(jnp.int32)


def set_ends(drawn, rng, least, largest):
    spot = [jax.random.randint(jax.random.fold_in(rng, axis), (), 0, length) for axis, length in enumerate(drawn.shape)]
    widest = drawn.shape.index(max(drawn.shape))
    beside = spot[:widest] + [(spot[widest] + 1) % drawn.shape[widest]] + spot[widest + 1:]
    return drawn.at[tuple(spot)].set(least).at[tuple(beside)].set(largest)


def steps_of(stream_key, shape, cuts, least, largest):
    def one(axis_at, shards_of):
        heights = jax.random.uniform(jax.random.fold_in(jax.random.fold_in(stream_key, 6), axis_at), (shards_of,), jnp.float32, least / len(cuts), largest / len(cuts))
        return jnp.repeat(jnp.exp(heights), shape[axis_at] // shards_of).reshape((-1,) + (1,) * (len(shape) - axis_at - 1))

    level = one(*cuts[0])
    for cut in cuts[1:]:
        level = level * one(*cut)
    return level


def normal_values(rng, extent, spread, reach, shards=(), kind=jnp.bfloat16):
    gain = steps_of(rng, extent, shards, -0.22, 0.18) if shards else 1.0
    drawn = jax.random.normal(rng, extent, jnp.float32) * spread * gain
    return jnp.minimum(jnp.maximum(drawn, -reach), reach).astype(kind)


def setup_inputs(seed: int = 0) -> dict:
    splits = jax.random.split(jax.random.key(seed), 8)
    queries = draw_queries(jax.random.fold_in(splits[7], 71), 0)
    keys_values = draw_keys_values(jax.random.fold_in(splits[7], 71), 0)
    cache_kv = normal_values(splits[2], (TOKENS, 2, KVH * HD), 1.0, 4.0, ((0, 8), (2, 4)))
    vertical_pages = draw_vertical_pages(jax.random.fold_in(splits[7], 71), 0)
    slash_shift = draw_slash_shift(jax.random.fold_in(splits[7], 71), 0)
    slash_live = set_ends((jax.random.randint(splits[5], (SHARDS, KVH, SLASH), 0, 4) < 3).astype(jnp.int32), jax.random.fold_in(splits[5], 1), 0, 1)
    out_proj = normal_values(splits[6], (HEADS * HD, D), (HEADS * HD) ** -0.5, 0.09375, ((0, 4),))
    return dict(queries=queries, keys_values=keys_values, cache_kv=cache_kv, vertical_pages=vertical_pages, slash_shift=slash_shift, slash_live=slash_live, out_proj=out_proj)


def reference(queries, keys_values, cache_kv, vertical_pages, slash_shift, slash_live, out_proj):
    group_heads = HEADS // KVH
    all_store = jnp.concatenate([cache_kv, keys_values], 0)

    def one_shard(shard_index):
        start_row = shard_index * ROWS
        query_block = lax.dynamic_slice_in_dim(queries, start_row, ROWS, 0).astype(jnp.float32)
        query_block = query_block.reshape(ROWS, KVH, group_heads, HD)
        local_block = lax.dynamic_slice_in_dim(keys_values, start_row, ROWS, 0)
        row_ids = lax.broadcasted_iota(jnp.int32, (ROWS, ROWS), 0)
        col_ids = lax.broadcasted_iota(jnp.int32, (ROWS, ROWS), 1)
        causal = row_ids >= col_ids
        group_outputs = []
        for group_index in range(KVH):
            low_col = group_index * HD
            high_col = low_col + HD
            distances = slash_shift[group_index]
            key_shards = (SHARDS + shard_index - distances).astype(jnp.int32)
            slash_block = jax.vmap(lambda shard_key: lax.dynamic_slice_in_dim(all_store, shard_key * ROWS, ROWS, 0))(key_shards)
            slash_block = slash_block[:, :, :, low_col:high_col].reshape(SLASH * ROWS, 2, HD)
            page_ids = vertical_pages[group_index]
            page_block = jax.vmap(lambda page_key: lax.dynamic_slice_in_dim(cache_kv, page_key * PAGE, PAGE, 0))(page_ids)
            page_block = page_block[:, :, :, low_col:high_col].reshape(VPAGES * PAGE, 2, HD)
            live_blocks = slash_live[shard_index, group_index] == 1
            clash = live_blocks[None, :] & (distances[None, :] > shard_index) & ((page_ids // PPS)[:, None] == key_shards[None, :])
            page_open = jnp.logical_not(jnp.any(clash, axis=1))
            column_open = jnp.concatenate([jnp.repeat(live_blocks, ROWS), jnp.repeat(page_open, PAGE)])
            visible = jnp.concatenate([causal, jnp.broadcast_to(column_open[None, :], (ROWS, column_open.shape[0]))], 1)
            all_keys = jnp.concatenate([local_block[:, :, low_col:high_col], slash_block, page_block], 0).astype(jnp.float32)
            scores = jnp.einsum("rgd,kd->grk", query_block[:, group_index], all_keys[:, 0, :]) * (HD ** -0.5)
            scores = jnp.where(visible[None], scores, -jnp.inf)
            row_max = jnp.max(scores, axis=2, keepdims=True)
            weights = jnp.exp(scores - row_max)
            row_total = jnp.sum(weights, axis=2, keepdims=True)
            weights_bf = (weights / row_total).astype(jnp.bfloat16).astype(jnp.float32)
            attended = jnp.einsum("grk,kd->rgd", weights_bf, all_keys[:, 1, :]).astype(jnp.bfloat16)
            group_outputs.append(attended)
        attended_all = jnp.stack(group_outputs, 1).reshape(ROWS, HEADS * HD)
        return jnp.dot(attended_all, out_proj, preferred_element_type=jnp.float32).astype(jnp.bfloat16)

    blocks = lax.map(one_shard, jnp.arange(SHARDS, dtype=jnp.int32))
    return blocks.reshape(TOKENS, D)
```

```python
import functools
import math

import jax
import jax.numpy as jnp
from jax import lax
from jax.experimental import pallas as pl
from jax.experimental.pallas import tpu as pltpu
from jax.sharding import PartitionSpec as P

PAGE = 128
LANES = 128
FAR = 1e30
TREE_MAX = 16


def swapped(value, axis, mask):
    count = lax.axis_size(axis)
    return lax.ppermute(value, axis, [(source, source ^ mask) for source in range(count)])


def passed_along(value, axis, steps):
    count = lax.axis_size(axis)
    return lax.ppermute(value, axis, [(source, (source + steps) % count) for source in range(count)])


def gathered(own, axis):
    blocks = {0: own}
    for mask in range(1, lax.axis_size(axis)):
        low = mask & -mask
        blocks[mask] = swapped(blocks[mask - low], axis, low)
    return [blocks[mask] for mask in range(len(blocks))]


def rotate(value, amount, shards):
    reduced = amount % shards
    for bit_number in range(max(1, (shards - 1).bit_length())):
        moved = passed_along(value, "seq", 1 << bit_number)
        value = jnp.where(reduced // (1 << bit_number) % 2 == 1, moved, value)
    return value


def attention_kernel(sizes, page_ref, shift_ref, live_ref, query_ref, own_ref, proj_ref, *rest):
    (shards, heads, head_width, slash_count, page_count, page_rows, per_shard, members, tree) = sizes
    store_count = (2 * shards - 1) if tree else (slash_count + page_count)
    stores = rest[:store_count]
    send_ref, keep_ref = rest[store_count : store_count + 2]
    raw, wide, keys, values, scores, weights, attended, proj, sems, proj_sem = rest[store_count + 2 :]
    me = lax.axis_index("seq")
    rows = query_ref.shape[0]
    proj_copy = pltpu.make_async_copy(proj_ref, proj, proj_sem)
    proj_copy.start()

    def slot(number):
        if number < slash_count:
            return raw.at[pl.ds(number * 2 * rows, 2 * rows)]
        first = slash_count * 2 * rows + (number - slash_count) * 2 * page_rows
        return raw.at[pl.ds(first, 2 * page_rows)]

    live = []
    for k in range(slash_count):
        distance = shift_ref[0, k]
        live.append((live_ref[0, k] == 1, distance > me, shards + me - distance))
        if not tree:
            pltpu.make_async_copy(stores[k], slot(k), sems.at[k]).start()
            continue
        differs = jnp.where(distance > me, shards + me - distance, me - distance) ^ me
        for mask in range(shards):
            for newer in (False, True):
                if newer and mask == 0:
                    continue
                source = stores[shards + mask - 1] if newer else stores[mask]

                @pl.when((differs == mask) & ((distance <= me) == newer))
                def _(source=source):
                    pltpu.make_async_copy(source, slot(k), sems.at[k]).start()

    opened = []
    for i in range(page_count):
        page = page_ref[0, i]
        owner = page // per_shard
        clash = functools.reduce(
            jnp.logical_or, [is_live & older & (source == owner) for is_live, older, source in live]
        )
        opened.append(jnp.logical_not(clash))
        number = slash_count + i
        if not tree:
            pltpu.make_async_copy(stores[number], slot(number), sems.at[number]).start()
            continue
        first = pl.multiple_of((page - owner * per_shard) * 2 * page_rows, 2 * page_rows)
        for mask in range(shards):

            @pl.when((owner ^ me) == mask)
            def _(mask=mask):
                pltpu.make_async_copy(
                    stores[mask].at[pl.ds(first, 2 * page_rows)], slot(number), sems.at[number]
                ).start()

    def split(source, first, count):
        wide[pl.ds(2 * first, 2 * count), :] = source[...].astype(jnp.float32)
        keys[pl.ds(first, count), :] = wide[pl.ds(2 * first, count, stride=2), :].astype(jnp.bfloat16)
        values[pl.ds(first, count), pl.ds(0, head_width)] = wide[
            pl.ds(2 * first + 1, count, stride=2), :
        ].astype(jnp.bfloat16)

    values[:, pl.ds(head_width, LANES)] = jnp.ones((values.shape[0], LANES), jnp.bfloat16)
    split(own_ref, 0, rows)
    chunks = [(0, rows, None)]
    first = rows
    for number in range(slash_count + page_count):
        count = rows if number < slash_count else page_rows
        place = slot(number)
        pltpu.make_async_copy(place, place, sems.at[number]).wait()
        split(place, first, count)
        flag = live[number][0] if number < slash_count else opened[number - slash_count]
        chunks.append((first, count, flag))
        first += count
    scale = head_width**-0.5 * math.log2(math.e)
    causal = lax.broadcasted_iota(jnp.int32, (rows, rows), 0) >= lax.broadcasted_iota(
        jnp.int32, (rows, rows), 1
    )

    def one_head(head, carry):
        column = pl.multiple_of(head * head_width, head_width)
        query = query_ref[:, pl.ds(column, head_width)]
        highest = None
        for start, count, flag in chunks:
            part = lax.dot_general(
                query,
                keys[pl.ds(start, count), :],
                (((1,), (1,)), ((), ())),
                preferred_element_type=jnp.float32,
            )
            if flag is None:
                part = jnp.where(causal, part, -FAR)
            scores[:, pl.ds(start, count)] = part
            top = functools.reduce(
                jnp.maximum, [part[:, at : at + LANES] for at in range(0, count, LANES)]
            )
            if flag is not None:
                top = jnp.where(flag, top, -FAR)
            highest = top if highest is None else jnp.maximum(highest, top)
        highest = jnp.max(highest, axis=1, keepdims=True)
        for start, count, flag in chunks:
            level = highest if flag is None else jnp.where(flag, highest, FAR)
            part = jnp.exp2((scores[:, pl.ds(start, count)] - level) * scale)
            weights[:, pl.ds(start, count)] = part.astype(jnp.bfloat16)
        total = jnp.dot(weights[...], values[...], preferred_element_type=jnp.float32)
        attended[:, pl.ds(column, head_width)] = (
            total[:, :head_width] / total[:, head_width:]
        ).astype(jnp.bfloat16)
        return carry

    lax.fori_loop(0, heads, one_head, 0)
    proj_copy.wait()
    mine = lax.axis_index("head")
    block = proj_ref.shape[1] // members
    for mask in range(members):
        column = pl.multiple_of((mine ^ mask) * block, block)
        term = jnp.dot(attended[...], proj[:, pl.ds(column, block)], preferred_element_type=jnp.float32)
        if mask % 2:
            send_ref[mask // 2] = term.astype(send_ref.dtype)
        else:
            keep_ref[mask // 2] = term


def body(queries, keys_values, cache_kv, vertical_pages, slash_shift, slash_live, out_proj):
    row_count = queries.shape[0]
    head_width = keys_values.shape[2]
    heads = queries.shape[1] // head_width
    shards = lax.axis_size("seq")
    members = lax.axis_size("head")
    slash_count = slash_shift.shape[1]
    page_count = vertical_pages.shape[1]
    per_shard = row_count // PAGE
    out_width = out_proj.shape[1]
    own = keys_values.reshape(2 * row_count, head_width)
    tree = shards <= TREE_MAX and shards & (shards - 1) == 0
    if tree:
        cache = cache_kv.reshape(2 * row_count, head_width)
        stores = gathered(cache, "seq") + gathered(own, "seq")[1:]
    else:
        own_shard = lax.axis_index("seq")
        stores = []
        for k in range(slash_count):
            distance = slash_shift[0, k]
            payload = jnp.where(own_shard < shards - distance, keys_values, cache_kv)
            stores.append(rotate(payload, distance, shards).reshape(2 * row_count, head_width))
        whole = lax.all_gather(cache_kv, "seq", axis=0, tiled=True)
        for i in range(page_count):
            page = lax.dynamic_slice_in_dim(whole, vertical_pages[0, i] * PAGE, PAGE, 0)
            stores.append(page.reshape(2 * PAGE, head_width))
    key_count = (1 + slash_count) * row_count + page_count * PAGE
    slots = slash_count + page_count
    sizes = (
        shards, heads, head_width, slash_count, page_count, PAGE, per_shard, members, tree,
    )
    anywhere = pl.BlockSpec(memory_space=pl.ANY)
    scalars = pl.BlockSpec(memory_space=pltpu.SMEM)
    vector = pl.BlockSpec(memory_space=pltpu.VMEM)
    block = out_width // members
    send, keep = pl.pallas_call(
        functools.partial(attention_kernel, sizes),
        out_shape=[
            jax.ShapeDtypeStruct((members // 2, row_count, block), jnp.bfloat16),
            jax.ShapeDtypeStruct((members // 2, row_count, block), jnp.float32),
        ],
        in_specs=[scalars] * 3 + [vector, vector, anywhere] + [anywhere] * len(stores),
        out_specs=[vector, vector],
        scratch_shapes=[
            pltpu.VMEM((2 * (key_count - row_count), head_width), jnp.bfloat16),
            pltpu.VMEM((2 * key_count, head_width), jnp.float32),
            pltpu.VMEM((key_count, head_width), jnp.bfloat16),
            pltpu.VMEM((key_count, head_width + LANES), jnp.bfloat16),
            pltpu.VMEM((row_count, key_count), jnp.float32),
            pltpu.VMEM((row_count, key_count), jnp.bfloat16),
            pltpu.VMEM((row_count, heads * head_width), jnp.bfloat16),
            pltpu.VMEM(out_proj.shape, jnp.bfloat16),
            pltpu.SemaphoreType.DMA((slots,)),
            pltpu.SemaphoreType.DMA,
        ],
        compiler_params=pltpu.CompilerParams(vmem_limit_bytes=24 << 20),
        cost_estimate=pl.CostEstimate(
            flops=4 * heads * row_count * key_count * head_width
            + 2 * row_count * heads * head_width * out_width,
            bytes_accessed=8 << 20,
            transcendentals=heads * row_count * key_count,
        ),
        name="attend",
    )(
        vertical_pages,
        slash_shift,
        slash_live.reshape(1, slash_count),
        queries,
        own,
        out_proj,
        *stores,
    )
    step = 1
    while step < members:
        keep = keep + swapped(send, "head", step).astype(jnp.float32)
        step *= 2
        if step < members:
            send = keep[1::2].astype(jnp.bfloat16)
            keep = keep[0::2]
    return keep[0].astype(jnp.bfloat16)


def solution(mesh):
    placed = (
        P("seq", "head"),
        P("seq", None, "head"),
        P("seq", None, "head"),
        P("head", None),
        P("head", None),
        P("seq", "head", None),
        P("head", None),
    )
    return jax.shard_map(
        body, mesh=mesh, in_specs=placed, out_specs=P("seq", "head"), check_vma=False
    )
```

```python
import functools
import math

import jax
import jax.numpy as jnp
from jax import lax
from jax.experimental import pallas as pl
from jax.experimental.pallas import tpu as pltpu
from jax.sharding import PartitionSpec as P

PAGE = 128
LANES = 128
FAR = 1e30
TREE_MAX = 16


def swapped(value, axis, mask):
    count = lax.axis_size(axis)
    return lax.ppermute(value, axis, [(source, source ^ mask) for source in range(count)])


def passed_along(value, axis, steps):
    count = lax.axis_size(axis)
    return lax.ppermute(value, axis, [(source, (source + steps) % count) for source in range(count)])


def gathered(own, axis):
    blocks = {0: own}
    for mask in range(1, lax.axis_size(axis)):
        low = mask & -mask
        blocks[mask] = swapped(blocks[mask - low], axis, low)
    return [blocks[mask] for mask in range(len(blocks))]


def rotate(value, amount, shards):
    reduced = amount % shards
    for bit_number in range(max(1, (shards - 1).bit_length())):
        moved = passed_along(value, "seq", 1 << bit_number)
        value = jnp.where(reduced // (1 << bit_number) % 2 == 1, moved, value)
    return value


def planar(source, wide, count):
    wide[pl.ds(0, 2 * count), :] = source[...].astype(jnp.float32)
    return (
        wide[pl.ds(0, count, stride=2), :].astype(jnp.bfloat16),
        wide[pl.ds(1, count, stride=2), :].astype(jnp.bfloat16),
    )


def stage_kernel(sizes, page_ref, shift_ref, live_ref, query_in, own_in, proj_in, *rest):
    table, query_out, proj_out, keys_out, values_out, raw, wide, sems = rest
    own_copy = pltpu.make_async_copy(own_in, raw, sems.at[0])
    query_copy = pltpu.make_async_copy(query_in, query_out, sems.at[1])
    proj_copy = pltpu.make_async_copy(proj_in, proj_out, sems.at[2])
    own_copy.start()
    query_copy.start()
    proj_copy.start()
    shards, per_shard = sizes["shards"], sizes["per_shard"]
    me = lax.axis_index("seq")
    seen = []
    for k in range(sizes["slash_count"]):
        distance = shift_ref[0, k]
        older = distance > me
        source = jnp.where(older, shards + me - distance, me - distance)
        live = live_ref[0, k] == 1
        seen.append((live & older, source))
        choice = (source ^ me) + jnp.where(older, 0, shards)
        table[0, 2 * k] = choice
        table[0, 2 * k + 1] = live.astype(jnp.int32)
    for i in range(sizes["page_count"]):
        page = page_ref[0, i]
        owner = page // per_shard
        clash = functools.reduce(
            jnp.logical_or, [active & (source == owner) for active, source in seen]
        )
        base = 2 * sizes["slash_count"] + 3 * i
        table[0, base] = owner ^ me
        table[0, base + 1] = page - owner * per_shard
        table[0, base + 2] = jnp.logical_not(clash).astype(jnp.int32)
    own_copy.wait()
    count = keys_out.shape[0]
    own_keys, own_values = planar(raw, wide, count)
    keys_out[...] = own_keys
    values_out[:, pl.ds(0, own_values.shape[1])] = own_values
    values_out[:, pl.ds(own_values.shape[1], LANES)] = jnp.ones((count, LANES), jnp.bfloat16)
    query_copy.wait()
    proj_copy.wait()


def attention_kernel(sizes, table, query_ref, proj_ref, own_keys, own_values, *rest):
    shards, heads, head_width = sizes["shards"], sizes["heads"], sizes["head_width"]
    slash_count, page_count = sizes["slash_count"], sizes["page_count"]
    page_rows, members, tree = sizes["page_rows"], sizes["members"], sizes["tree"]
    store_count = (2 * shards - 1) if tree else (slash_count + page_count)
    stores = rest[:store_count]
    send_ref, keep_ref = rest[store_count : store_count + 2]
    raw, wide, keys, values, scores, weights, attended, sems = rest[store_count + 2 :]
    rows = query_ref.shape[0]

    def slot(number):
        if number < slash_count:
            return raw.at[pl.ds(number * 2 * rows, 2 * rows)]
        first = slash_count * 2 * rows + (number - slash_count) * 2 * page_rows
        return raw.at[pl.ds(first, 2 * page_rows)]

    for k in range(slash_count):
        if not tree:
            pltpu.make_async_copy(stores[k], slot(k), sems.at[k]).start()
            continue
        for choice in range(2 * shards):
            if choice == shards:
                continue
            source = stores[choice] if choice < shards else stores[choice - 1]

            @pl.when(table[0, 2 * k] == choice)
            def _(source=source):
                pltpu.make_async_copy(source, slot(k), sems.at[k]).start()

    for i in range(page_count):
        number = slash_count + i
        base = 2 * slash_count + 3 * i
        if not tree:
            pltpu.make_async_copy(stores[number], slot(number), sems.at[number]).start()
            continue
        first = pl.multiple_of(table[0, base + 1] * (2 * page_rows), 2 * page_rows)
        for mask in range(shards):

            @pl.when(table[0, base] == mask)
            def _(mask=mask):
                pltpu.make_async_copy(
                    stores[mask].at[pl.ds(first, 2 * page_rows)], slot(number), sems.at[number]
                ).start()

    keys[pl.ds(0, rows), :] = own_keys[...]
    values[pl.ds(0, rows), :] = own_values[...]
    chunks = [(0, rows, None)]
    first = rows
    values[pl.ds(rows, values.shape[0] - rows), pl.ds(head_width, LANES)] = jnp.ones(
        (values.shape[0] - rows, LANES), jnp.bfloat16
    )
    for number in range(slash_count + page_count):
        count = rows if number < slash_count else page_rows
        place = slot(number)
        pltpu.make_async_copy(place, place, sems.at[number]).wait()
        new_keys, new_values = planar(place, wide.at[pl.ds(2 * first, 2 * count)], count)
        keys[pl.ds(first, count), :] = new_keys
        values[pl.ds(first, count), pl.ds(0, head_width)] = new_values
        at = 2 * number + 1 if number < slash_count else 2 * slash_count + 3 * (number - slash_count) + 2
        chunks.append((first, count, table[0, at] == 1))
        first += count
    scale = head_width**-0.5 * math.log2(math.e)
    causal = lax.broadcasted_iota(jnp.int32, (rows, rows), 0) >= lax.broadcasted_iota(
        jnp.int32, (rows, rows), 1
    )

    def score(head, chunk, highest):
        start, count, flag = chunk
        part = lax.dot_general(
            query_ref[:, pl.ds(head * head_width, head_width)],
            keys[pl.ds(start, count), :],
            (((1,), (1,)), ((), ())),
            preferred_element_type=jnp.float32,
        )
        if flag is None:
            part = jnp.where(causal, part, -FAR)
        scores[head % 2, :, pl.ds(start, count)] = part
        top = functools.reduce(
            jnp.maximum, [part[:, at : at + LANES] for at in range(0, count, LANES)]
        )
        if flag is not None:
            top = jnp.where(flag, top, -FAR)
        return top if highest is None else jnp.maximum(highest, top)

    def weigh(head, chunk, highest):
        start, count, flag = chunk
        level = highest if flag is None else jnp.where(flag, highest, FAR)
        part = jnp.exp2((scores[head % 2, :, pl.ds(start, count)] - level) * scale)
        weights[head % 2, :, pl.ds(start, count)] = part.astype(jnp.bfloat16)

    running = None
    for chunk in chunks:
        running = score(0, chunk, running)
    for head in range(heads):
        highest = jnp.max(running, axis=1, keepdims=True)
        running = None
        for chunk in chunks:
            if head + 1 < heads:
                running = score(head + 1, chunk, running)
            weigh(head, chunk, highest)
        total = jnp.dot(weights[head % 2], values[...], preferred_element_type=jnp.float32)
        attended[:, pl.ds(head * head_width, head_width)] = (
            total[:, :head_width] / total[:, head_width:]
        ).astype(jnp.bfloat16)

    mine = lax.axis_index("head")
    block = proj_ref.shape[1] // members
    for mask in range(members):
        column = pl.multiple_of((mine ^ mask) * block, block)
        term = jnp.dot(
            attended[...], proj_ref[:, pl.ds(column, block)], preferred_element_type=jnp.float32
        )
        if mask % 2:
            send_ref[mask // 2] = term.astype(send_ref.dtype)
        else:
            keep_ref[mask // 2] = term


def body(queries, keys_values, cache_kv, vertical_pages, slash_shift, slash_live, out_proj):
    row_count = queries.shape[0]
    head_width = keys_values.shape[2]
    heads = queries.shape[1] // head_width
    shards = lax.axis_size("seq")
    members = lax.axis_size("head")
    slash_count = slash_shift.shape[1]
    page_count = vertical_pages.shape[1]
    per_shard = row_count // PAGE
    out_width = out_proj.shape[1]
    own = keys_values.reshape(2 * row_count, head_width)
    tree = shards <= TREE_MAX and shards & (shards - 1) == 0
    if tree:
        cache = cache_kv.reshape(2 * row_count, head_width)
        stores = gathered(cache, "seq") + gathered(own, "seq")[1:]
    else:
        own_shard = lax.axis_index("seq")
        stores = []
        for k in range(slash_count):
            distance = slash_shift[0, k]
            payload = jnp.where(own_shard < shards - distance, keys_values, cache_kv)
            stores.append(rotate(payload, distance, shards).reshape(2 * row_count, head_width))
        whole = lax.all_gather(cache_kv, "seq", axis=0, tiled=True)
        for i in range(page_count):
            page = lax.dynamic_slice_in_dim(whole, vertical_pages[0, i] * PAGE, PAGE, 0)
            stores.append(page.reshape(2 * PAGE, head_width))
    key_count = (1 + slash_count) * row_count + page_count * PAGE
    sizes = dict(
        shards=shards, heads=heads, head_width=head_width, slash_count=slash_count,
        page_count=page_count, page_rows=PAGE, per_shard=per_shard, members=members, tree=tree,
    )
    hbm = pl.BlockSpec(memory_space=pltpu.HBM)
    scalars = pl.BlockSpec(memory_space=pltpu.SMEM)
    vector = pl.BlockSpec(memory_space=pltpu.VMEM)
    block = out_width // members
    table, query_near, proj_near, own_keys, own_values = pl.pallas_call(
        functools.partial(stage_kernel, sizes),
        out_shape=[
            jax.ShapeDtypeStruct((1, 2 * slash_count + 3 * page_count), jnp.int32),
            jax.ShapeDtypeStruct(queries.shape, queries.dtype),
            jax.ShapeDtypeStruct(out_proj.shape, out_proj.dtype),
            jax.ShapeDtypeStruct((row_count, head_width), jnp.bfloat16),
            jax.ShapeDtypeStruct((row_count, head_width + LANES), jnp.bfloat16),
        ],
        in_specs=[scalars] * 3 + [hbm] * 3,
        out_specs=[scalars] + [vector] * 4,
        scratch_shapes=[
            pltpu.VMEM((2 * row_count, head_width), jnp.bfloat16),
            pltpu.VMEM((2 * row_count, head_width), jnp.float32),
            pltpu.SemaphoreType.DMA((3,)),
        ],
        compiler_params=pltpu.CompilerParams(vmem_limit_bytes=8 << 20),
        cost_estimate=pl.CostEstimate(flops=0, bytes_accessed=10 << 20, transcendentals=0),
        name="stage",
    )(
        vertical_pages,
        slash_shift,
        slash_live.reshape(1, slash_count),
        queries,
        own,
        out_proj,
    )
    send, keep = pl.pallas_call(
        functools.partial(attention_kernel, sizes),
        out_shape=[
            jax.ShapeDtypeStruct((members // 2, row_count, block), jnp.bfloat16),
            jax.ShapeDtypeStruct((members // 2, row_count, block), jnp.float32),
        ],
        in_specs=[scalars] + [vector] * (4 + len(stores)),
        out_specs=[vector, vector],
        scratch_shapes=[
            pltpu.VMEM((2 * (key_count - row_count), head_width), jnp.bfloat16),
            pltpu.VMEM((2 * key_count, head_width), jnp.float32),
            pltpu.VMEM((key_count, head_width), jnp.bfloat16),
            pltpu.VMEM((key_count, head_width + LANES), jnp.bfloat16),
            pltpu.VMEM((2, row_count, key_count), jnp.float32),
            pltpu.VMEM((2, row_count, key_count), jnp.bfloat16),
            pltpu.VMEM((row_count, heads * head_width), jnp.bfloat16),
            pltpu.SemaphoreType.DMA((slash_count + page_count,)),
        ],
        compiler_params=pltpu.CompilerParams(vmem_limit_bytes=32 << 20),
        cost_estimate=pl.CostEstimate(
            flops=4 * heads * row_count * key_count * head_width
            + 2 * row_count * heads * head_width * out_width,
            bytes_accessed=8 << 20,
            transcendentals=heads * row_count * key_count,
        ),
        name="attend",
    )(table, query_near, proj_near, own_keys, own_values, *stores)
    step = 1
    while step < members:
        keep = keep + swapped(send, "head", step).astype(jnp.float32)
        step *= 2
        if step < members:
            send = keep[1::2].astype(jnp.bfloat16)
            keep = keep[0::2]
    return keep[0].astype(jnp.bfloat16)


def solution(mesh):
    placed = (
        P("seq", "head"),
        P("seq", None, "head"),
        P("seq", None, "head"),
        P("head", None),
        P("head", None),
        P("seq", "head", None),
        P("head", None),
    )
    return jax.shard_map(
        body, mesh=mesh, in_specs=placed, out_specs=P("seq", "head"), check_vma=False
    )
```

```python
import functools
import math

import jax
import jax.numpy as jnp
from jax import lax
from jax.experimental import pallas as pl
from jax.experimental.pallas import tpu as pltpu
from jax.sharding import PartitionSpec as P

PAGE = 128
LANES = 128
FAR = 1e30
TREE_MAX = 16


def swapped(value, axis, mask):
    count = lax.axis_size(axis)
    return lax.ppermute(value, axis, [(source, source ^ mask) for source in range(count)])


def passed_along(value, axis, steps):
    count = lax.axis_size(axis)
    return lax.ppermute(value, axis, [(source, (source + steps) % count) for source in range(count)])


def gathered(first_hops, axis, unit):
    blocks = {}
    for mask in range(1, lax.axis_size(axis) // unit):
        low = mask & -mask
        source = blocks[mask - low] if mask > low else first_hops[low]
        blocks[mask] = swapped(source, axis, low * unit)
    return [blocks[mask] for mask in range(1, len(blocks) + 1)]


def rotate(value, amount, shards):
    reduced = amount % shards
    for bit_number in range(max(1, (shards - 1).bit_length())):
        moved = passed_along(value, "seq", 1 << bit_number)
        value = jnp.where(reduced // (1 << bit_number) % 2 == 1, moved, value)
    return value


def decoded(sizes, table, me):
    shards, per_shard = sizes["shards"], sizes["per_shard"]
    slash_count, page_count = sizes["slash_count"], sizes["page_count"]
    slashes, pages = [], []
    for k in range(slash_count):
        distance = table[page_count + k]
        older = distance > me
        source = jnp.where(older, shards + me - distance, me - distance)
        slashes.append((source ^ me, older, table[page_count + slash_count + k] == 1))
    for i in range(page_count):
        owner = table[i] // per_shard
        clash = functools.reduce(
            jnp.logical_or,
            [live & older & (bits == (owner ^ me)) for bits, older, live in slashes],
        )
        pages.append((owner ^ me, table[i] - owner * per_shard, jnp.logical_not(clash)))
    return slashes, pages


def pick_kernel(sizes, table, *rest):
    pieces, slots = rest[:-1], rest[-1]
    piece = sizes["piece"]
    _, pages = decoded(sizes, table, lax.axis_index("seq"))
    for i, (bits, place, _) in enumerate(pages):
        for mask, source in enumerate(pieces):

            @pl.when((bits >> 1) == mask)
            def _(source=source):
                first = pl.multiple_of(place * piece, piece)
                slots[pl.ds(i * piece, piece), :] = source[pl.ds(first, piece), :]


def merge_kernel(sizes, table, mine, other, merged):
    piece = sizes["piece"]
    _, pages = decoded(sizes, table, lax.axis_index("seq"))
    for i, (bits, _, _) in enumerate(pages):
        here = pl.ds(i * piece, piece)
        merged[here, :] = mine[here, :]

        @pl.when((bits & 1) == 1)
        def _():
            merged[here, :] = other[here, :]


def stage_kernel(query_in, proj_in, own_in, cache_in, *rest):
    sems = rest[-1]
    copies = [
        pltpu.make_async_copy(source, place, sems.at[at])
        for at, (source, place) in enumerate(zip((query_in, proj_in, own_in, cache_in), rest[:-1]))
    ]
    for copy in copies:
        copy.start()
    for copy in copies:
        copy.wait()


def attention_kernel(sizes, table, query_ref, proj_ref, own_ref, *rest):
    shards, heads, head_width = sizes["shards"], sizes["heads"], sizes["head_width"]
    slash_count, page_count = sizes["slash_count"], sizes["page_count"]
    page_rows, members, tree = sizes["page_rows"], sizes["members"], sizes["tree"]
    piece = sizes["piece"]
    block_count = shards if tree else slash_count
    piece_count = shards // 2 if tree else page_count
    blocks = rest[:block_count]
    pieces = rest[block_count : block_count + piece_count]
    rest = rest[block_count + piece_count :]
    send_ref, keep_ref, wide, keys, values, scores, weights, attended = rest
    rows = query_ref.shape[0]
    slashes, pages = decoded(sizes, table, lax.axis_index("seq"))
    wide[pl.ds(0, 2 * rows), :] = own_ref[...].astype(jnp.float32)
    chunks = [(0, rows, None)]
    first = rows
    for k, (bits, _, live) in enumerate(slashes):
        here = pl.ds(2 * first, 2 * rows)
        if tree:
            for mask in range(shards):

                @pl.when(bits == mask)
                def _(mask=mask):
                    wide[here, :] = blocks[mask][...].astype(jnp.float32)
        else:
            wide[here, :] = blocks[k][...].astype(jnp.float32)
        chunks.append((first, rows, live))
        first += rows
    for i, (bits, _, is_open) in enumerate(pages):
        if tree:
            for mask in range(piece_count):
                at = pl.multiple_of(2 * first + (mask ^ (bits >> 1)) * piece, piece)
                wide[pl.ds(at, piece), :] = pieces[mask][pl.ds(i * piece, piece), :].astype(
                    jnp.float32
                )
        else:
            wide[pl.ds(2 * first, 2 * page_rows), :] = pieces[i][...].astype(jnp.float32)
        chunks.append((first, page_rows, is_open))
        first += page_rows
    keys[...] = wide[pl.ds(0, first, stride=2), :].astype(jnp.bfloat16)
    values[:, pl.ds(0, head_width)] = wide[pl.ds(1, first, stride=2), :].astype(jnp.bfloat16)
    values[:, pl.ds(head_width, LANES)] = jnp.ones((first, LANES), jnp.bfloat16)
    scale = head_width**-0.5 * math.log2(math.e)
    causal = lax.broadcasted_iota(jnp.int32, (rows, rows), 0) >= lax.broadcasted_iota(
        jnp.int32, (rows, rows), 1
    )

    def score(head, chunk, highest):
        start, count, flag = chunk
        part = lax.dot_general(
            query_ref[:, pl.ds(head * head_width, head_width)],
            keys[pl.ds(start, count), :],
            (((1,), (1,)), ((), ())),
            preferred_element_type=jnp.float32,
        )
        if flag is None:
            part = jnp.where(causal, part, -FAR)
        scores[head % 2, :, pl.ds(start, count)] = part
        top = functools.reduce(
            jnp.maximum, [part[:, at : at + LANES] for at in range(0, count, LANES)]
        )
        if flag is not None:
            top = jnp.where(flag, top, -FAR)
        return top if highest is None else jnp.maximum(highest, top)

    def weigh(head, chunk, highest):
        start, count, flag = chunk
        level = highest if flag is None else jnp.where(flag, highest, FAR)
        part = jnp.exp2((scores[head % 2, :, pl.ds(start, count)] - level) * scale)
        weights[head % 2, :, pl.ds(start, count)] = part.astype(jnp.bfloat16)

    running = None
    for chunk in chunks:
        running = score(0, chunk, running)
    for head in range(heads):
        highest = jnp.max(running, axis=1, keepdims=True)
        running = None
        for chunk in chunks:
            if head + 1 < heads:
                running = score(head + 1, chunk, running)
            weigh(head, chunk, highest)
        total = jnp.dot(weights[head % 2], values[...], preferred_element_type=jnp.float32)
        attended[:, pl.ds(head * head_width, head_width)] = (
            total[:, :head_width] / total[:, head_width:]
        ).astype(jnp.bfloat16)

    mine = lax.axis_index("head")
    block = proj_ref.shape[1] // members
    for mask in range(members):
        column = pl.multiple_of((mine ^ mask) * block, block)
        term = jnp.dot(
            attended[...], proj_ref[:, pl.ds(column, block)], preferred_element_type=jnp.float32
        )
        if mask % 2:
            send_ref[mask // 2] = term.astype(send_ref.dtype)
        else:
            keep_ref[mask // 2] = term


def body(queries, keys_values, cache_kv, vertical_pages, slash_shift, slash_live, out_proj):
    row_count = queries.shape[0]
    head_width = keys_values.shape[2]
    heads = queries.shape[1] // head_width
    shards = lax.axis_size("seq")
    members = lax.axis_size("head")
    slash_count = slash_shift.shape[1]
    page_count = vertical_pages.shape[1]
    per_shard = row_count // PAGE
    out_width = out_proj.shape[1]
    own = keys_values.reshape(2 * row_count, head_width)
    cache = cache_kv.reshape(2 * row_count, head_width)
    tree = 4 <= shards <= TREE_MAX and shards & (shards - 1) == 0
    piece = 2 * PAGE // (shards // 2) if tree else 0
    sizes = dict(
        shards=shards, heads=heads, head_width=head_width, slash_count=slash_count,
        page_count=page_count, page_rows=PAGE, per_shard=per_shard, members=members, tree=tree,
        piece=piece,
    )
    scalars = pl.BlockSpec(memory_space=pltpu.SMEM)
    vector = pl.BlockSpec(memory_space=pltpu.VMEM)
    table = jnp.concatenate([vertical_pages[0], slash_shift[0], slash_live[0, 0]])
    own_shard = lax.axis_index("seq")
    if tree:
        near = cache.reshape(per_shard, shards // 2, piece, head_width)
        near = [
            near[:, mask].reshape(per_shard * piece, head_width) for mask in range(shards // 2)
        ]
        pieces = near[:1] + [
            swapped(near[mask], "seq", 2 * mask) for mask in range(1, shards // 2)
        ]
        first_hops = {}
        bit = 1
        while bit < shards:
            first_hops[bit] = jnp.where(own_shard & bit == 0, own, cache)
            bit *= 2
        blocks = [cache] + gathered(first_hops, "seq", 1)
        slot_shape = jax.ShapeDtypeStruct((page_count * piece, head_width), jnp.bfloat16)
        small = dict(
            out_shape=slot_shape,
            out_specs=vector,
            compiler_params=pltpu.CompilerParams(vmem_limit_bytes=2 << 20),
            cost_estimate=pl.CostEstimate(flops=0, bytes_accessed=4 << 20, transcendentals=0),
        )
        mine = pl.pallas_call(
            functools.partial(pick_kernel, sizes),
            in_specs=[scalars] + [vector] * len(pieces),
            name="pick",
            **small,
        )(table, *pieces)
        merged = pl.pallas_call(
            functools.partial(merge_kernel, sizes),
            in_specs=[scalars, vector, vector],
            name="merge",
            **small,
        )(table, mine, swapped(mine, "seq", 1))
        hops = {1 << bit: merged for bit in range(shards.bit_length())}
        pieces = [merged] + gathered(hops, "seq", 2)
    else:
        blocks, pieces = [], []
        for k in range(slash_count):
            distance = slash_shift[0, k]
            payload = jnp.where(own_shard < shards - distance, keys_values, cache_kv)
            blocks.append(rotate(payload, distance, shards).reshape(2 * row_count, head_width))
        whole = lax.all_gather(cache_kv, "seq", axis=0, tiled=True)
        for i in range(page_count):
            page = lax.dynamic_slice_in_dim(whole, vertical_pages[0, i] * PAGE, PAGE, 0)
            pieces.append(page.reshape(2 * PAGE, head_width))
    near = [queries, out_proj, own, cache]
    near = pl.pallas_call(
        stage_kernel,
        out_shape=[jax.ShapeDtypeStruct(value.shape, value.dtype) for value in near],
        in_specs=[vector] * len(near),
        out_specs=[vector] * len(near),
        scratch_shapes=[pltpu.SemaphoreType.DMA((len(near),))],
        compiler_params=pltpu.CompilerParams(vmem_limit_bytes=1 << 20),
        cost_estimate=pl.CostEstimate(flops=0, bytes_accessed=10 << 20, transcendentals=0),
        name="stage",
    )(*near)
    if tree:
        blocks[0] = near[3]
    key_count = (1 + slash_count) * row_count + page_count * PAGE
    block = out_width // members
    send, keep = pl.pallas_call(
        functools.partial(attention_kernel, sizes),
        out_shape=[
            jax.ShapeDtypeStruct((members // 2, row_count, block), jnp.bfloat16),
            jax.ShapeDtypeStruct((members // 2, row_count, block), jnp.float32),
        ],
        in_specs=[scalars] + [vector] * (3 + len(blocks) + len(pieces)),
        out_specs=[vector, vector],
        scratch_shapes=[
            pltpu.VMEM((2 * key_count, head_width), jnp.float32),
            pltpu.VMEM((key_count, head_width), jnp.bfloat16),
            pltpu.VMEM((key_count, head_width + LANES), jnp.bfloat16),
            pltpu.VMEM((2, row_count, key_count), jnp.float32),
            pltpu.VMEM((2, row_count, key_count), jnp.bfloat16),
            pltpu.VMEM((row_count, heads * head_width), jnp.bfloat16),
        ],
        compiler_params=pltpu.CompilerParams(vmem_limit_bytes=32 << 20),
        cost_estimate=pl.CostEstimate(
            flops=4 * heads * row_count * key_count * head_width
            + 2 * row_count * heads * head_width * out_width,
            bytes_accessed=8 << 20,
            transcendentals=heads * row_count * key_count,
        ),
        name="attend",
    )(table, *near[:3], *blocks, *pieces)
    step = 1
    while step < members:
        keep = keep + swapped(send, "head", step).astype(jnp.float32)
        step *= 2
        if step < members:
            send = keep[1::2].astype(jnp.bfloat16)
            keep = keep[0::2]
    return keep[0].astype(jnp.bfloat16)


def solution(mesh):
    placed = (
        P("seq", "head"),
        P("seq", None, "head"),
        P("seq", None, "head"),
        P("head", None),
        P("head", None),
        P("seq", "head", None),
        P("head", None),
    )
    return jax.shard_map(
        body, mesh=mesh, in_specs=placed, out_specs=P("seq", "head"), check_vma=False
    )
```

```python
import functools
import math

import jax
import jax.numpy as jnp
from jax import lax
from jax.experimental import pallas as pl
from jax.experimental.pallas import tpu as pltpu
from jax.sharding import PartitionSpec as P


PAGE = 128
LANES = 128
FAR = 1e30
TREE_MAX = 16


def swapped(value, axis, mask):
    count = lax.axis_size(axis)
    return lax.ppermute(value, axis, [(source, source ^ mask) for source in range(count)])


def passed_along(value, axis, steps):
    count = lax.axis_size(axis)
    return lax.ppermute(value, axis, [(source, (source + steps) % count) for source in range(count)])


def gathered(first_hops, axis, count):
    blocks = {}
    for mask in range(1, count):
        low = mask & -mask
        source = blocks[mask - low] if mask > low else first_hops[low]
        blocks[mask] = swapped(source, axis, low)
    return [blocks[mask] for mask in range(1, count)]


def rotate(value, amount, shards):
    reduced = amount % shards
    for bit_number in range(max(1, (shards - 1).bit_length())):
        moved = passed_along(value, "seq", 1 << bit_number)
        value = jnp.where(reduced // (1 << bit_number) % 2 == 1, moved, value)
    return value


def decoded(sizes, table, me):
    shards, per_shard = sizes["shards"], sizes["per_shard"]
    slash_count, page_count = sizes["slash_count"], sizes["page_count"]
    slashes, pages = [], []
    for k in range(slash_count):
        distance = table[0, page_count + k]
        older = distance > me
        source = jnp.where(older, shards + me - distance, me - distance)
        slashes.append((source ^ me, older, table[0, page_count + slash_count + k] == 1))
    for i in range(page_count):
        owner = table[0, i] // per_shard
        clash = functools.reduce(
            jnp.logical_or,
            [live & older & (bits == (owner ^ me)) for bits, older, live in slashes],
        )
        pages.append((owner ^ me, table[0, i] - owner * per_shard, jnp.logical_not(clash)))
    return slashes, pages


def open_kernel(sizes, own_in, cache_in, *rest):
    shards, per_shard, piece = sizes["shards"], sizes["per_shard"], sizes["piece"]
    own_near, cache_near, sems = rest[0], rest[1], rest[-1]
    hop_count = shards.bit_length() - 1
    hops, pieces = rest[2 : 2 + hop_count], rest[2 + hop_count : -1]
    copies = [
        pltpu.make_async_copy(own_in, own_near, sems.at[0]),
        pltpu.make_async_copy(cache_in, cache_near, sems.at[1]),
    ]
    for copy in copies:
        copy.start()
    for copy in copies:
        copy.wait()
    me = lax.axis_index("seq")
    for number, hop in enumerate(hops):
        upper = (me >> number) & 1

        @pl.when(upper == 0)
        def _(hop=hop):
            hop[...] = own_near[...]

        @pl.when(upper == 1)
        def _(hop=hop):
            hop[...] = cache_near[...]

    for mask, place in enumerate(pieces):
        for at in range(per_shard):
            first = (at * len(pieces) + mask) * piece
            place[pl.ds(at * piece, piece), :] = cache_near[pl.ds(first, piece), :]


def stage_kernel(query_in, page_in, shift_in, live_in, query_near, table, *rest):
    page_near, shift_near, live_near, sems = rest
    ints = (page_near, shift_near, live_near)
    copies = [
        pltpu.make_async_copy(source, place, sems.at[at])
        for at, (source, place) in enumerate(
            [(page_in, page_near), (shift_in, shift_near), (live_in, live_near)]
            + [(query_in, query_near)]
        )
    ]
    for copy in copies:
        copy.start()
    for copy in copies[:3]:
        copy.wait()
    at = 0
    for part in ints:
        for entry in range(part.shape[1]):
            table[0, at] = part[0, entry]
            at += 1
    copies[3].wait()


def pick_kernel(sizes, table, *rest):
    pieces, slots = rest[:-1], rest[-1]
    piece = sizes["piece"]
    _, pages = decoded(sizes, table, lax.axis_index("seq"))
    for i, (bits, place, _) in enumerate(pages):
        for mask, source in enumerate(pieces):

            @pl.when((bits & (len(pieces) - 1)) == mask)
            def _(source=source):
                first = pl.multiple_of(place * piece, piece)
                slots[pl.ds(i * piece, piece), :] = source[pl.ds(first, piece), :]


def merge_kernel(sizes, table, mine, other, merged):
    piece = sizes["piece"]
    _, pages = decoded(sizes, table, lax.axis_index("seq"))
    for i, (bits, _, _) in enumerate(pages):
        here = pl.ds(i * piece, piece)
        far = bits >= sizes["shards"] // 2

        @pl.when(far)
        def _(here=here):
            merged[here, :] = other[here, :]

        @pl.when(jnp.logical_not(far))
        def _(here=here):
            merged[here, :] = mine[here, :]


def attention_kernel(sizes, table, query_ref, proj_ref, own_ref, *rest):
    shards, heads, head_width = sizes["shards"], sizes["heads"], sizes["head_width"]
    slash_count, page_count = sizes["slash_count"], sizes["page_count"]
    page_rows, members, tree = sizes["page_rows"], sizes["members"], sizes["tree"]
    piece = sizes["piece"]
    block_count = shards if tree else slash_count
    piece_count = shards // 2 if tree else page_count
    blocks = rest[:block_count]
    pieces = rest[block_count : block_count + piece_count]
    rest = rest[block_count + piece_count :]
    send_ref, keep_ref, wide, keys, values, scores, weights, attended, proj, proj_sem = rest
    proj_copy = pltpu.make_async_copy(proj_ref, proj, proj_sem)
    proj_copy.start()
    rows = query_ref.shape[0]
    slashes, pages = decoded(sizes, table, lax.axis_index("seq"))
    wide[pl.ds(0, 2 * rows), :] = own_ref[...].astype(jnp.float32)
    chunks = [(0, rows, None)]
    first = rows
    for k, (bits, _, live) in enumerate(slashes):
        here = pl.ds(2 * first, 2 * rows)
        if tree:
            for mask in range(shards):

                @pl.when(bits == mask)
                def _(mask=mask):
                    wide[here, :] = blocks[mask][...].astype(jnp.float32)
        else:
            wide[here, :] = blocks[k][...].astype(jnp.float32)
        chunks.append((first, rows, live))
        first += rows
    for i, (bits, _, is_open) in enumerate(pages):
        if tree:
            for mask in range(piece_count):
                at = pl.multiple_of(2 * first + ((mask ^ bits) & (piece_count - 1)) * piece, piece)
                wide[pl.ds(at, piece), :] = pieces[mask][pl.ds(i * piece, piece), :].astype(
                    jnp.float32
                )
        else:
            wide[pl.ds(2 * first, 2 * page_rows), :] = pieces[i][...].astype(jnp.float32)
        chunks.append((first, page_rows, is_open))
        first += page_rows
    keys[...] = wide[pl.ds(0, first, stride=2), :].astype(jnp.bfloat16)
    values[:, pl.ds(0, head_width)] = wide[pl.ds(1, first, stride=2), :].astype(jnp.bfloat16)
    values[:, pl.ds(head_width, LANES)] = jnp.ones((first, LANES), jnp.bfloat16)
    scale = head_width**-0.5 * math.log2(math.e)
    causal = lax.broadcasted_iota(jnp.int32, (rows, rows), 0) >= lax.broadcasted_iota(
        jnp.int32, (rows, rows), 1
    )

    def score(head, chunk, highest):
        start, count, flag = chunk
        part = lax.dot_general(
            query_ref[:, pl.ds(head * head_width, head_width)],
            keys[pl.ds(start, count), :],
            (((1,), (1,)), ((), ())),
            preferred_element_type=jnp.float32,
        )
        if flag is None:
            part = jnp.where(causal, part, -FAR)
        scores[head % 2, :, pl.ds(start, count)] = part
        top = functools.reduce(
            jnp.maximum, [part[:, at : at + LANES] for at in range(0, count, LANES)]
        )
        if flag is not None:
            top = jnp.where(flag, top, -FAR)
        return top if highest is None else jnp.maximum(highest, top)

    def weigh(head, chunk, highest):
        start, count, flag = chunk
        level = highest if flag is None else jnp.where(flag, highest, FAR)
        part = jnp.exp2((scores[head % 2, :, pl.ds(start, count)] - level) * scale)
        weights[head % 2, :, pl.ds(start, count)] = part.astype(jnp.bfloat16)

    running = None
    for chunk in chunks:
        running = score(0, chunk, running)
    for head in range(heads):
        highest = jnp.max(running, axis=1, keepdims=True)
        running = None
        for chunk in chunks:
            if head + 1 < heads:
                running = score(head + 1, chunk, running)
            weigh(head, chunk, highest)
        total = jnp.dot(weights[head % 2], values[...], preferred_element_type=jnp.float32)
        attended[:, pl.ds(head * head_width, head_width)] = (
            total[:, :head_width] / total[:, head_width:]
        ).astype(jnp.bfloat16)

    proj_copy.wait()
    mine = lax.axis_index("head")
    block = proj_ref.shape[1] // members
    for mask in range(members):
        column = pl.multiple_of((mine ^ mask) * block, block)
        term = jnp.dot(
            attended[...], proj[:, pl.ds(column, block)], preferred_element_type=jnp.float32
        )
        if mask % 2:
            send_ref[mask // 2] = term.astype(send_ref.dtype)
        else:
            keep_ref[mask // 2] = term


def body(queries, keys_values, cache_kv, vertical_pages, slash_shift, slash_live, out_proj):
    row_count = queries.shape[0]
    head_width = keys_values.shape[2]
    heads = queries.shape[1] // head_width
    shards = lax.axis_size("seq")
    members = lax.axis_size("head")
    slash_count = slash_shift.shape[1]
    page_count = vertical_pages.shape[1]
    per_shard = row_count // PAGE
    out_width = out_proj.shape[1]
    own = keys_values.reshape(2 * row_count, head_width)
    cache = cache_kv.reshape(2 * row_count, head_width)
    tree = is_tree(shards)
    piece = 2 * PAGE // (shards // 2) if tree else 0
    sizes = dict(
        shards=shards, heads=heads, head_width=head_width, slash_count=slash_count,
        page_count=page_count, page_rows=PAGE, per_shard=per_shard, members=members, tree=tree,
        piece=piece,
    )
    scalars = pl.BlockSpec(memory_space=pltpu.SMEM)
    vector = pl.BlockSpec(memory_space=pltpu.VMEM)
    hbm = pl.BlockSpec(memory_space=pltpu.HBM)
    far = functools.partial(pltpu.with_memory_space_constraint, memory_space=pltpu.HBM)
    lists = [vertical_pages, slash_shift, slash_live.reshape(1, slash_count)]
    table_size = sum(part.shape[1] for part in lists)
    queries, table = pl.pallas_call(
        stage_kernel,
        out_shape=[
            jax.ShapeDtypeStruct(queries.shape, queries.dtype),
            jax.ShapeDtypeStruct((1, table_size), jnp.int32),
        ],
        in_specs=[hbm] * 4,
        out_specs=[vector, scalars],
        scratch_shapes=[pltpu.SMEM(part.shape, jnp.int32) for part in lists]
        + [pltpu.SemaphoreType.DMA((4,))],
        compiler_params=pltpu.CompilerParams(vmem_limit_bytes=1 << 20),
        cost_estimate=pl.CostEstimate(flops=0, bytes_accessed=2 << 20, transcendentals=0),
        name="stage",
    )(*map(far, [queries] + lists))
    own_shard = lax.axis_index("seq")
    if tree:
        half = shards // 2
        bits = [1 << number for number in range(shards.bit_length() - 1)]
        block_shape = jax.ShapeDtypeStruct(own.shape, own.dtype)
        piece_shape = jax.ShapeDtypeStruct((per_shard * piece, head_width), own.dtype)
        opened = pl.pallas_call(
            functools.partial(open_kernel, sizes),
            out_shape=[block_shape] * (2 + len(bits)) + [piece_shape] * half,
            in_specs=[hbm] * 2,
            out_specs=[vector] * (2 + len(bits) + half),
            scratch_shapes=[pltpu.SemaphoreType.DMA((2,))],
            compiler_params=pltpu.CompilerParams(vmem_limit_bytes=1 << 20),
            cost_estimate=pl.CostEstimate(flops=0, bytes_accessed=1 << 20, transcendentals=0),
            name="open",
        )(far(own), far(cache))
        own, cache = opened[:2]
        near = opened[2 + len(bits) :]
        pieces = [near[0]] + [swapped(near[mask], "seq", mask) for mask in range(1, half)]
        first_hops = dict(zip(bits, opened[2 : 2 + len(bits)]))
        blocks = [cache] + gathered(first_hops, "seq", shards)
        slot_shape = jax.ShapeDtypeStruct((page_count * piece, head_width), jnp.bfloat16)
        small = dict(
            out_shape=slot_shape,
            out_specs=vector,
            compiler_params=pltpu.CompilerParams(vmem_limit_bytes=2 << 20),
            cost_estimate=pl.CostEstimate(flops=0, bytes_accessed=4 << 20, transcendentals=0),
        )
        mine = pl.pallas_call(
            functools.partial(pick_kernel, sizes),
            in_specs=[scalars] + [vector] * len(pieces),
            name="pick",
            **small,
        )(table, *pieces)
        merged = pl.pallas_call(
            functools.partial(merge_kernel, sizes),
            in_specs=[scalars, vector, vector],
            name="merge",
            **small,
        )(table, mine, swapped(mine, "seq", half))
        pieces = [merged] + gathered(dict.fromkeys(bits, merged), "seq", half)
    else:
        blocks, pieces = [], []
        for k in range(slash_count):
            distance = slash_shift[0, k]
            payload = jnp.where(own_shard < shards - distance, keys_values, cache_kv)
            blocks.append(rotate(payload, distance, shards).reshape(2 * row_count, head_width))
        whole = lax.all_gather(cache_kv, "seq", axis=0, tiled=True)
        for i in range(page_count):
            page = lax.dynamic_slice_in_dim(whole, vertical_pages[0, i] * PAGE, PAGE, 0)
            pieces.append(page.reshape(2 * PAGE, head_width))
    key_count = (1 + slash_count) * row_count + page_count * PAGE
    block = out_width // members
    send, keep = pl.pallas_call(
        functools.partial(attention_kernel, sizes),
        out_shape=[
            jax.ShapeDtypeStruct((members // 2, row_count, block), jnp.bfloat16),
            jax.ShapeDtypeStruct((members // 2, row_count, block), jnp.float32),
        ],
        in_specs=[scalars, vector, hbm] + [vector] * (1 + len(blocks) + len(pieces)),
        out_specs=[vector, vector],
        scratch_shapes=[
            pltpu.VMEM((2 * key_count, head_width), jnp.float32),
            pltpu.VMEM((key_count, head_width), jnp.bfloat16),
            pltpu.VMEM((key_count, head_width + LANES), jnp.bfloat16),
            pltpu.VMEM((2, row_count, key_count), jnp.float32),
            pltpu.VMEM((2, row_count, key_count), jnp.bfloat16),
            pltpu.VMEM((row_count, heads * head_width), jnp.bfloat16),
            pltpu.VMEM(out_proj.shape, out_proj.dtype),
            pltpu.SemaphoreType.DMA,
        ],
        compiler_params=pltpu.CompilerParams(vmem_limit_bytes=32 << 20),
        cost_estimate=pl.CostEstimate(
            flops=4 * heads * row_count * key_count * head_width
            + 2 * row_count * heads * head_width * out_width,
            bytes_accessed=8 << 20,
            transcendentals=heads * row_count * key_count,
        ),
        name="attend",
    )(table, queries, far(out_proj), own, *blocks, *pieces)
    step = 1
    while step < members:
        keep = keep + swapped(send, "head", step).astype(jnp.float32)
        step *= 2
        if step < members:
            send = keep[1::2].astype(jnp.bfloat16)
            keep = keep[0::2]
    return keep[0].astype(jnp.bfloat16)


def is_tree(shards):
    return 4 <= shards <= TREE_MAX and shards & (shards - 1) == 0


def solution(mesh):
    placed = (
        P("seq", "head"),
        P("seq", None, "head"),
        P("seq", None, "head"),
        P("head", None),
        P("head", None),
        P("seq", "head", None),
        P("head", None),
    )


    step = jax.shard_map(
        body, mesh=mesh, in_specs=placed, out_specs=P("seq", "head"), check_vma=False
    )
    if not is_tree(mesh.shape["seq"]):
        return step
    return step
```

```python
import functools
import math

import jax
import jax.numpy as jnp
from jax import lax
from jax.experimental import pallas as pl
from jax.experimental.pallas import tpu as pltpu
from jax.sharding import PartitionSpec as P


PAGE = 128
LANES = 128
FAR = 1e30
TREE_MAX = 16


def swapped(value, axis, mask):
    count = lax.axis_size(axis)
    return lax.ppermute(value, axis, [(source, source ^ mask) for source in range(count)])


def passed_along(value, axis, steps):
    count = lax.axis_size(axis)
    return lax.ppermute(value, axis, [(source, (source + steps) % count) for source in range(count)])


def gathered(first_hops, axis, count, high_first):
    blocks = {}
    for mask in range(1, count):
        last = mask & -mask if high_first else 1 << (mask.bit_length() - 1)
        source = blocks[mask - last] if mask > last else first_hops[last]
        blocks[mask] = swapped(source, axis, last)
    return [blocks[mask] for mask in range(1, count)]


def rotate(value, amount, shards):
    reduced = amount % shards
    for bit_number in range(max(1, (shards - 1).bit_length())):
        moved = passed_along(value, "seq", 1 << bit_number)
        value = jnp.where(reduced // (1 << bit_number) % 2 == 1, moved, value)
    return value


def decoded(sizes, table, me):
    shards, per_shard = sizes["shards"], sizes["per_shard"]
    slash_count, page_count = sizes["slash_count"], sizes["page_count"]
    slashes, pages = [], []
    for k in range(slash_count):
        distance = table[0, page_count + k]
        older = distance > me
        source = jnp.where(older, shards + me - distance, me - distance)
        slashes.append((source ^ me, older, table[0, page_count + slash_count + k] == 1))
    for i in range(page_count):
        owner = table[0, i] // per_shard
        clash = functools.reduce(
            jnp.logical_or,
            [live & older & (bits == (owner ^ me)) for bits, older, live in slashes],
        )
        pages.append((owner ^ me, table[0, i] - owner * per_shard, jnp.logical_not(clash)))
    return slashes, pages


def fill_table(table, lists):
    at = 0
    for part in lists:
        for entry in range(part.shape[1]):
            table[0, at] = part[0, entry]
            at += 1


def table_kernel(page_in, shift_in, live_in, table, *rest):
    lists, sems = rest[:3], rest[3]
    copies = [
        pltpu.make_async_copy(source, place, sems.at[at])
        for at, (source, place) in enumerate(zip((page_in, shift_in, live_in), lists))
    ]
    for copy in copies:
        copy.start()
    for copy in copies:
        copy.wait()
    fill_table(table, lists)


def open_kernel(sizes, own_in, cache_in, page_in, shift_in, live_in, *rest):
    shards, per_shard, piece = sizes["shards"], sizes["per_shard"], sizes["piece"]
    own_near, cache_near, table = rest[:3]
    lists, sems = rest[-4:-1], rest[-1]
    hop_count = shards.bit_length() - 1
    hops, pieces = rest[3 : 3 + hop_count], rest[3 + hop_count : -4]
    sources = (own_in, cache_in, page_in, shift_in, live_in)
    copies = [
        pltpu.make_async_copy(source, place, sems.at[at])
        for at, (source, place) in enumerate(zip(sources, (own_near, cache_near) + tuple(lists)))
    ]
    for copy in copies:
        copy.start()
    for copy in copies:
        copy.wait()
    fill_table(table, lists)
    me = lax.axis_index("seq")
    for number, hop in enumerate(hops):
        upper = (me >> number) & 1

        @pl.when(upper == 0)
        def _(hop=hop):
            hop[...] = own_near[...]

        @pl.when(upper == 1)
        def _(hop=hop):
            hop[...] = cache_near[...]

    for mask, place in enumerate(pieces):
        for at in range(per_shard):
            first = (at * len(pieces) + mask) * piece
            place[pl.ds(at * piece, piece), :] = cache_near[pl.ds(first, piece), :]


def stage_kernel(query_in, query_near, sem):
    copy = pltpu.make_async_copy(query_in, query_near, sem)
    copy.start()
    copy.wait()


def pick_kernel(sizes, table, *rest):
    pieces, slots = rest[:-1], rest[-1]
    piece = sizes["piece"]
    _, pages = decoded(sizes, table, lax.axis_index("seq"))
    for i, (bits, place, _) in enumerate(pages):
        for mask, source in enumerate(pieces):

            @pl.when((bits & (len(pieces) - 1)) == mask)
            def _(source=source):
                first = pl.multiple_of(place * piece, piece)
                slots[pl.ds(i * piece, piece), :] = source[pl.ds(first, piece), :]


def merge_kernel(sizes, table, mine, other, merged):
    piece = sizes["piece"]
    _, pages = decoded(sizes, table, lax.axis_index("seq"))
    for i, (bits, _, _) in enumerate(pages):
        here = pl.ds(i * piece, piece)
        far = bits >= sizes["shards"] // 2

        @pl.when(far)
        def _(here=here):
            merged[here, :] = other[here, :]

        @pl.when(jnp.logical_not(far))
        def _(here=here):
            merged[here, :] = mine[here, :]


def attention_kernel(sizes, table, query_ref, proj_ref, own_ref, *rest):
    shards, heads, head_width = sizes["shards"], sizes["heads"], sizes["head_width"]
    slash_count, page_count = sizes["slash_count"], sizes["page_count"]
    page_rows, members, tree = sizes["page_rows"], sizes["members"], sizes["tree"]
    piece = sizes["piece"]
    block_count = shards if tree else slash_count
    piece_count = shards // 2 if tree else page_count
    blocks = rest[:block_count]
    pieces = rest[block_count : block_count + piece_count]
    rest = rest[block_count + piece_count :]
    send_ref, keep_ref, wide, keys, values, scores, weights, attended, proj, proj_sem = rest
    proj_copy = pltpu.make_async_copy(proj_ref, proj, proj_sem)
    proj_copy.start()
    rows = query_ref.shape[0]
    slashes, pages = decoded(sizes, table, lax.axis_index("seq"))
    wide[pl.ds(0, 2 * rows), :] = own_ref[...].astype(jnp.float32)
    chunks = [(0, rows, None)]
    first = rows
    for k, (bits, _, live) in enumerate(slashes):
        here = pl.ds(2 * first, 2 * rows)
        if tree:
            for mask in range(shards):

                @pl.when(bits == mask)
                def _(mask=mask):
                    wide[here, :] = blocks[mask][...].astype(jnp.float32)
        else:
            wide[here, :] = blocks[k][...].astype(jnp.float32)
        chunks.append((first, rows, live))
        first += rows
    for i, (bits, _, is_open) in enumerate(pages):
        if tree:
            for mask in range(piece_count):
                at = pl.multiple_of(2 * first + ((mask ^ bits) & (piece_count - 1)) * piece, piece)
                wide[pl.ds(at, piece), :] = pieces[mask][pl.ds(i * piece, piece), :].astype(
                    jnp.float32
                )
        else:
            wide[pl.ds(2 * first, 2 * page_rows), :] = pieces[i][...].astype(jnp.float32)
        chunks.append((first, page_rows, is_open))
        first += page_rows
    keys[...] = wide[pl.ds(0, first, stride=2), :].astype(jnp.bfloat16)
    values[:, pl.ds(0, head_width)] = wide[pl.ds(1, first, stride=2), :].astype(jnp.bfloat16)
    values[:, pl.ds(head_width, LANES)] = jnp.ones((first, LANES), jnp.bfloat16)
    scale = head_width**-0.5 * math.log2(math.e)
    causal = lax.broadcasted_iota(jnp.int32, (rows, rows), 0) >= lax.broadcasted_iota(
        jnp.int32, (rows, rows), 1
    )

    def score(head, chunk, highest):
        start, count, flag = chunk
        part = lax.dot_general(
            query_ref[:, pl.ds(head * head_width, head_width)],
            keys[pl.ds(start, count), :],
            (((1,), (1,)), ((), ())),
            preferred_element_type=jnp.float32,
        )
        if flag is None:
            part = jnp.where(causal, part, -FAR)
        scores[head % 2, :, pl.ds(start, count)] = part
        top = functools.reduce(
            jnp.maximum, [part[:, at : at + LANES] for at in range(0, count, LANES)]
        )
        if flag is not None:
            top = jnp.where(flag, top, -FAR)
        return top if highest is None else jnp.maximum(highest, top)

    def weigh(head, chunk, highest):
        start, count, flag = chunk
        level = highest if flag is None else jnp.where(flag, highest, FAR)
        part = jnp.exp2((scores[head % 2, :, pl.ds(start, count)] - level) * scale)
        weights[head % 2, :, pl.ds(start, count)] = part.astype(jnp.bfloat16)

    running = None
    for chunk in chunks:
        running = score(0, chunk, running)
    for head in range(heads):
        highest = jnp.max(running, axis=1, keepdims=True)
        running = None
        for chunk in chunks:
            if head + 1 < heads:
                running = score(head + 1, chunk, running)
            weigh(head, chunk, highest)
        total = jnp.dot(weights[head % 2], values[...], preferred_element_type=jnp.float32)
        attended[:, pl.ds(head * head_width, head_width)] = (
            total[:, :head_width] / total[:, head_width:]
        ).astype(jnp.bfloat16)

    proj_copy.wait()
    mine = lax.axis_index("head")
    block = proj_ref.shape[1] // members
    for mask in range(members):
        column = pl.multiple_of((mine ^ mask) * block, block)
        term = jnp.dot(
            attended[...], proj[:, pl.ds(column, block)], preferred_element_type=jnp.float32
        )
        if mask % 2:
            send_ref[mask // 2] = term.astype(send_ref.dtype)
        else:
            keep_ref[mask // 2] = term


def body(queries, keys_values, cache_kv, vertical_pages, slash_shift, slash_live, out_proj):
    row_count = queries.shape[0]
    head_width = keys_values.shape[2]
    heads = queries.shape[1] // head_width
    shards = lax.axis_size("seq")
    members = lax.axis_size("head")
    slash_count = slash_shift.shape[1]
    page_count = vertical_pages.shape[1]
    per_shard = row_count // PAGE
    out_width = out_proj.shape[1]
    own = keys_values.reshape(2 * row_count, head_width)
    cache = cache_kv.reshape(2 * row_count, head_width)
    tree = is_tree(shards)
    piece = 2 * PAGE // (shards // 2) if tree else 0
    sizes = dict(
        shards=shards, heads=heads, head_width=head_width, slash_count=slash_count,
        page_count=page_count, page_rows=PAGE, per_shard=per_shard, members=members, tree=tree,
        piece=piece,
    )
    scalars = pl.BlockSpec(memory_space=pltpu.SMEM)
    vector = pl.BlockSpec(memory_space=pltpu.VMEM)
    hbm = pl.BlockSpec(memory_space=pltpu.HBM)
    far = functools.partial(pltpu.with_memory_space_constraint, memory_space=pltpu.HBM)
    lists = [vertical_pages, slash_shift, slash_live.reshape(1, slash_count)]
    table_size = sum(part.shape[1] for part in lists)
    table_shape = jax.ShapeDtypeStruct((1, table_size), jnp.int32)
    list_scratch = [pltpu.SMEM(part.shape, jnp.int32) for part in lists]
    queries = pl.pallas_call(
        stage_kernel,
        out_shape=jax.ShapeDtypeStruct(queries.shape, queries.dtype),
        in_specs=[hbm],
        out_specs=vector,
        scratch_shapes=[pltpu.SemaphoreType.DMA],
        compiler_params=pltpu.CompilerParams(vmem_limit_bytes=1 << 20),
        cost_estimate=pl.CostEstimate(flops=0, bytes_accessed=2 << 20, transcendentals=0),
        name="stage",
    )(far(queries))
    own_shard = lax.axis_index("seq")
    if tree:
        half = shards // 2
        bits = [1 << number for number in range(shards.bit_length() - 1)]
        block_shape = jax.ShapeDtypeStruct(own.shape, own.dtype)
        piece_shape = jax.ShapeDtypeStruct((per_shard * piece, head_width), own.dtype)
        opened = pl.pallas_call(
            functools.partial(open_kernel, sizes),
            out_shape=[block_shape] * 2
            + [table_shape]
            + [block_shape] * len(bits)
            + [piece_shape] * half,
            in_specs=[hbm] * 5,
            out_specs=[vector] * 2 + [scalars] + [vector] * (len(bits) + half),
            scratch_shapes=list_scratch + [pltpu.SemaphoreType.DMA((5,))],
            compiler_params=pltpu.CompilerParams(vmem_limit_bytes=1 << 20),
            cost_estimate=pl.CostEstimate(flops=0, bytes_accessed=1 << 20, transcendentals=0),
            name="open",
        )(*map(far, [own, cache] + lists))
        own, cache, table = opened[:3]
        near = opened[3 + len(bits) :]
        pieces = [near[0]] + [swapped(near[mask], "seq", mask) for mask in range(1, half)]
        first_hops = dict(zip(bits, opened[3 : 3 + len(bits)]))
        blocks = [cache] + gathered(first_hops, "seq", shards, True)
        slot_shape = jax.ShapeDtypeStruct((page_count * piece, head_width), jnp.bfloat16)
        small = dict(
            out_shape=slot_shape,
            out_specs=vector,
            compiler_params=pltpu.CompilerParams(vmem_limit_bytes=2 << 20),
            cost_estimate=pl.CostEstimate(flops=0, bytes_accessed=4 << 20, transcendentals=0),
        )
        mine = pl.pallas_call(
            functools.partial(pick_kernel, sizes),
            in_specs=[scalars] + [vector] * len(pieces),
            name="pick",
            **small,
        )(table, *pieces)
        merged = pl.pallas_call(
            functools.partial(merge_kernel, sizes),
            in_specs=[scalars, vector, vector],
            name="merge",
            **small,
        )(table, mine, swapped(mine, "seq", half))
        pieces = [merged] + gathered(dict.fromkeys(bits, merged), "seq", half, False)
    else:
        table = pl.pallas_call(
            table_kernel,
            out_shape=table_shape,
            in_specs=[hbm] * 3,
            out_specs=scalars,
            scratch_shapes=list_scratch + [pltpu.SemaphoreType.DMA((3,))],
            name="table",
        )(*map(far, lists))
        blocks, pieces = [], []
        for k in range(slash_count):
            distance = slash_shift[0, k]
            payload = jnp.where(own_shard < shards - distance, keys_values, cache_kv)
            blocks.append(rotate(payload, distance, shards).reshape(2 * row_count, head_width))
        whole = lax.all_gather(cache_kv, "seq", axis=0, tiled=True)
        for i in range(page_count):
            page = lax.dynamic_slice_in_dim(whole, vertical_pages[0, i] * PAGE, PAGE, 0)
            pieces.append(page.reshape(2 * PAGE, head_width))
    key_count = (1 + slash_count) * row_count + page_count * PAGE
    block = out_width // members
    send, keep = pl.pallas_call(
        functools.partial(attention_kernel, sizes),
        out_shape=[
            jax.ShapeDtypeStruct((members // 2, row_count, block), jnp.bfloat16),
            jax.ShapeDtypeStruct((members // 2, row_count, block), jnp.float32),
        ],
        in_specs=[scalars, vector, hbm] + [vector] * (1 + len(blocks) + len(pieces)),
        out_specs=[vector, vector],
        scratch_shapes=[
            pltpu.VMEM((2 * key_count, head_width), jnp.float32),
            pltpu.VMEM((key_count, head_width), jnp.bfloat16),
            pltpu.VMEM((key_count, head_width + LANES), jnp.bfloat16),
            pltpu.VMEM((2, row_count, key_count), jnp.float32),
            pltpu.VMEM((2, row_count, key_count), jnp.bfloat16),
            pltpu.VMEM((row_count, heads * head_width), jnp.bfloat16),
            pltpu.VMEM(out_proj.shape, out_proj.dtype),
            pltpu.SemaphoreType.DMA,
        ],
        compiler_params=pltpu.CompilerParams(vmem_limit_bytes=32 << 20),
        cost_estimate=pl.CostEstimate(
            flops=4 * heads * row_count * key_count * head_width
            + 2 * row_count * heads * head_width * out_width,
            bytes_accessed=8 << 20,
            transcendentals=heads * row_count * key_count,
        ),
        name="attend",
    )(table, queries, far(out_proj), own, *blocks, *pieces)
    step = 1
    while step < members:
        keep = keep + swapped(send, "head", step).astype(jnp.float32)
        step *= 2
        if step < members:
            send = keep[1::2].astype(jnp.bfloat16)
            keep = keep[0::2]
    return keep[0].astype(jnp.bfloat16)


def is_tree(shards):
    return 4 <= shards <= TREE_MAX and shards & (shards - 1) == 0


def solution(mesh):
    placed = (
        P("seq", "head"),
        P("seq", None, "head"),
        P("seq", None, "head"),
        P("head", None),
        P("head", None),
        P("seq", "head", None),
        P("head", None),
    )


    step = jax.shard_map(
        body, mesh=mesh, in_specs=placed, out_specs=P("seq", "head"), check_vma=False
    )
    if not is_tree(mesh.shape["seq"]):
        return step
    return step
```

```python
import functools
import math

import jax
import jax.numpy as jnp
from jax import lax
from jax.experimental import pallas as pl
from jax.experimental.pallas import tpu as pltpu
from jax.sharding import PartitionSpec as P


PAGE = 128
LANES = 128
FAR = 1e30
TREE_MAX = 16


def swapped(value, axis, mask):
    count = lax.axis_size(axis)
    return lax.ppermute(value, axis, [(source, source ^ mask) for source in range(count)])


def passed_along(value, axis, steps):
    count = lax.axis_size(axis)
    return lax.ppermute(value, axis, [(source, (source + steps) % count) for source in range(count)])


def gathered(first_hops, axis, rows):
    blocks = {}
    for mask in range(1, lax.axis_size(axis)):
        low = mask & -mask
        source = blocks[mask - low][:rows] if mask > low else first_hops[low]
        blocks[mask] = swapped(source, axis, low)
    return [blocks[mask] for mask in range(1, len(blocks) + 1)]


def rotate(value, amount, shards):
    reduced = amount % shards
    for bit_number in range(max(1, (shards - 1).bit_length())):
        moved = passed_along(value, "seq", 1 << bit_number)
        value = jnp.where(reduced // (1 << bit_number) % 2 == 1, moved, value)
    return value


def decoded(sizes, table, me):
    shards, per_shard = sizes["shards"], sizes["per_shard"]
    slash_count, page_count = sizes["slash_count"], sizes["page_count"]
    slashes, pages = [], []
    for k in range(slash_count):
        distance = table[0, page_count + k]
        older = distance > me
        source = jnp.where(older, shards + me - distance, me - distance)
        slashes.append((source ^ me, older, table[0, page_count + slash_count + k] == 1))
    for i in range(page_count):
        owner = table[0, i] // per_shard
        clash = functools.reduce(
            jnp.logical_or,
            [live & older & (bits == (owner ^ me)) for bits, older, live in slashes],
        )
        pages.append((owner ^ me, table[0, i] - owner * per_shard, jnp.logical_not(clash)))
    return slashes, pages


def open_kernel(sizes, own_in, cache_in, own_near, cache_near, *rest):
    shards, per_shard, piece = sizes["shards"], sizes["per_shard"], sizes["piece"]
    sems, half = rest[-1], shards // 2
    hop_count = shards.bit_length() - 1
    hops, alone = rest[:hop_count], list(rest[hop_count:-1])
    copies = [
        pltpu.make_async_copy(own_in, own_near, sems.at[0]),
        pltpu.make_async_copy(cache_in, cache_near, sems.at[1]),
    ]
    for copy in copies:
        copy.start()
    for copy in copies:
        copy.wait()
    me = lax.axis_index("seq")
    block = pl.ds(0, own_near.shape[0])
    for number, hop in enumerate(hops):
        upper = (me >> number) & 1

        @pl.when(upper == 0)
        def _(hop=hop):
            hop[block, :] = own_near[...]

        @pl.when(upper == 1)
        def _(hop=hop):
            hop[block, :] = cache_near[...]

    for mask in range(half):
        if mask and mask & (mask - 1) == 0:
            place, base = hops[mask.bit_length() - 1], own_near.shape[0]
        else:
            place, base = alone.pop(0), 0
        for at in range(per_shard):
            first = (at * half + mask) * piece
            place[pl.ds(base + at * piece, piece), :] = cache_near[pl.ds(first, piece), :]


def stage_kernel(query_in, page_in, shift_in, live_in, query_near, table, *rest):
    lists, sems = rest[:3], rest[3]
    sources = (page_in, shift_in, live_in, query_in)
    copies = [
        pltpu.make_async_copy(source, place, sems.at[at])
        for at, (source, place) in enumerate(zip(sources, tuple(lists) + (query_near,)))
    ]
    for copy in copies:
        copy.start()
    for copy in copies[:3]:
        copy.wait()
    at = 0
    for part in lists:
        for entry in range(part.shape[1]):
            table[0, at] = part[0, entry]
            at += 1
    copies[3].wait()


def pick_kernel(sizes, table, *rest):
    pieces, slots = rest[:-1], rest[-1]
    piece = sizes["piece"]
    _, pages = decoded(sizes, table, lax.axis_index("seq"))
    for i, (bits, place, _) in enumerate(pages):
        for mask, source in enumerate(pieces):

            @pl.when((bits & (len(pieces) - 1)) == mask)
            def _(source=source):
                base = source.shape[0] - sizes["per_shard"] * piece
                first = pl.multiple_of(base + place * piece, piece)
                slots[pl.ds(i * piece, piece), :] = source[pl.ds(first, piece), :]


def merge_kernel(sizes, table, mine, other, merged):
    piece = sizes["piece"]
    _, pages = decoded(sizes, table, lax.axis_index("seq"))
    for i, (bits, _, _) in enumerate(pages):
        here = pl.ds(i * piece, piece)
        far = bits >= sizes["shards"] // 2

        @pl.when(far)
        def _(here=here):
            merged[here, :] = other[here, :]

        @pl.when(jnp.logical_not(far))
        def _(here=here):
            merged[here, :] = mine[here, :]


def attention_kernel(sizes, table, query_ref, proj_ref, own_ref, *rest):
    shards, heads, head_width = sizes["shards"], sizes["heads"], sizes["head_width"]
    slash_count, page_count = sizes["slash_count"], sizes["page_count"]
    page_rows, members, tree = sizes["page_rows"], sizes["members"], sizes["tree"]
    piece = sizes["piece"]
    block_count = shards if tree else slash_count
    piece_count = shards.bit_length() - 1 if tree else page_count
    half = shards // 2
    blocks = rest[:block_count]
    pieces = rest[block_count : block_count + piece_count]
    rest = rest[block_count + piece_count :]
    send_ref, keep_ref, wide, keys, values, scores, weights, attended, proj, proj_sem = rest
    proj_copy = pltpu.make_async_copy(proj_ref, proj, proj_sem)
    proj_copy.start()
    rows = query_ref.shape[0]
    slashes, pages = decoded(sizes, table, lax.axis_index("seq"))
    wide[pl.ds(0, 2 * rows), :] = own_ref[...].astype(jnp.float32)
    chunks = [(0, rows, None)]
    first = rows
    for k, (bits, _, live) in enumerate(slashes):
        here = pl.ds(2 * first, 2 * rows)
        if tree:
            for mask in range(shards):

                @pl.when(bits == mask)
                def _(mask=mask):
                    wide[here, :] = blocks[mask][pl.ds(0, 2 * rows), :].astype(jnp.float32)
        else:
            wide[here, :] = blocks[k][...].astype(jnp.float32)
        chunks.append((first, rows, live))
        first += rows
    for i, (bits, _, is_open) in enumerate(pages):
        if tree:
            for mask in range(half):
                at = pl.multiple_of(2 * first + ((mask ^ bits) & (half - 1)) * piece, piece)
                top = 1 << (mask.bit_length() - 1) if mask else 0
                start = ((mask - top) * page_count + i) * piece
                source = pieces[mask.bit_length()][pl.ds(start, piece), :]
                wide[pl.ds(at, piece), :] = source.astype(jnp.float32)
        else:
            wide[pl.ds(2 * first, 2 * page_rows), :] = pieces[i][...].astype(jnp.float32)
        chunks.append((first, page_rows, is_open))
        first += page_rows
    keys[...] = wide[pl.ds(0, first, stride=2), :].astype(jnp.bfloat16)
    values[:, pl.ds(0, head_width)] = wide[pl.ds(1, first, stride=2), :].astype(jnp.bfloat16)
    values[:, pl.ds(head_width, LANES)] = jnp.ones((first, LANES), jnp.bfloat16)
    scale = head_width**-0.5 * math.log2(math.e)
    causal = lax.broadcasted_iota(jnp.int32, (rows, rows), 0) >= lax.broadcasted_iota(
        jnp.int32, (rows, rows), 1
    )

    def score(head, chunk, highest):
        start, count, flag = chunk
        part = lax.dot_general(
            query_ref[:, pl.ds(head * head_width, head_width)],
            keys[pl.ds(start, count), :],
            (((1,), (1,)), ((), ())),
            preferred_element_type=jnp.float32,
        )
        if flag is None:
            part = jnp.where(causal, part, -FAR)
        scores[head % 2, :, pl.ds(start, count)] = part
        top = functools.reduce(
            jnp.maximum, [part[:, at : at + LANES] for at in range(0, count, LANES)]
        )
        if flag is not None:
            top = jnp.where(flag, top, -FAR)
        return top if highest is None else jnp.maximum(highest, top)

    def weigh(head, chunk, highest):
        start, count, flag = chunk
        level = highest if flag is None else jnp.where(flag, highest, FAR)
        part = jnp.exp2((scores[head % 2, :, pl.ds(start, count)] - level) * scale)
        weights[head % 2, :, pl.ds(start, count)] = part.astype(jnp.bfloat16)

    running = None
    for chunk in chunks:
        running = score(0, chunk, running)
    for head in range(heads):
        highest = jnp.max(running, axis=1, keepdims=True)
        running = None
        for chunk in chunks:
            if head + 1 < heads:
                running = score(head + 1, chunk, running)
            weigh(head, chunk, highest)
        total = jnp.dot(weights[head % 2], values[...], preferred_element_type=jnp.float32)
        attended[:, pl.ds(head * head_width, head_width)] = (
            total[:, :head_width] / total[:, head_width:]
        ).astype(jnp.bfloat16)

    proj_copy.wait()
    mine = lax.axis_index("head")
    block = proj_ref.shape[1] // members
    for mask in range(members):
        column = pl.multiple_of((mine ^ mask) * block, block)
        term = jnp.dot(
            attended[...], proj[:, pl.ds(column, block)], preferred_element_type=jnp.float32
        )
        if mask % 2:
            send_ref[mask // 2] = term.astype(send_ref.dtype)
        else:
            keep_ref[mask // 2] = term


def body(queries, keys_values, cache_kv, vertical_pages, slash_shift, slash_live, out_proj):
    row_count = queries.shape[0]
    head_width = keys_values.shape[2]
    heads = queries.shape[1] // head_width
    shards = lax.axis_size("seq")
    members = lax.axis_size("head")
    slash_count = slash_shift.shape[1]
    page_count = vertical_pages.shape[1]
    per_shard = row_count // PAGE
    out_width = out_proj.shape[1]
    own = keys_values.reshape(2 * row_count, head_width)
    cache = cache_kv.reshape(2 * row_count, head_width)
    tree = is_tree(shards)
    piece = 2 * PAGE // (shards // 2) if tree else 0
    sizes = dict(
        shards=shards, heads=heads, head_width=head_width, slash_count=slash_count,
        page_count=page_count, page_rows=PAGE, per_shard=per_shard, members=members, tree=tree,
        piece=piece,
    )
    scalars = pl.BlockSpec(memory_space=pltpu.SMEM)
    vector = pl.BlockSpec(memory_space=pltpu.VMEM)
    hbm = pl.BlockSpec(memory_space=pltpu.HBM)
    far = functools.partial(pltpu.with_memory_space_constraint, memory_space=pltpu.HBM)
    lists = [vertical_pages, slash_shift, slash_live.reshape(1, slash_count)]
    table_size = sum(part.shape[1] for part in lists)
    queries, table = pl.pallas_call(
        stage_kernel,
        out_shape=[
            jax.ShapeDtypeStruct(queries.shape, queries.dtype),
            jax.ShapeDtypeStruct((1, table_size), jnp.int32),
        ],
        in_specs=[hbm] * 4,
        out_specs=[vector, scalars],
        scratch_shapes=[pltpu.SMEM(part.shape, jnp.int32) for part in lists]
        + [pltpu.SemaphoreType.DMA((4,))],
        compiler_params=pltpu.CompilerParams(vmem_limit_bytes=1 << 20),
        cost_estimate=pl.CostEstimate(flops=0, bytes_accessed=2 << 20, transcendentals=0),
        name="stage",
    )(*map(far, [queries] + lists))
    own_shard = lax.axis_index("seq")
    if tree:
        half = shards // 2
        bits = [1 << number for number in range(shards.bit_length() - 1)]
        block_shape = jax.ShapeDtypeStruct(own.shape, own.dtype)
        piece_rows = per_shard * piece
        alone = [mask for mask in range(1, half) if mask & (mask - 1)]
        extra = [
            jax.ShapeDtypeStruct((own.shape[0] + (piece_rows if bit < half else 0), head_width), own.dtype)
            for bit in bits
        ]
        piece_shape = jax.ShapeDtypeStruct((piece_rows, head_width), own.dtype)
        opened = pl.pallas_call(
            functools.partial(open_kernel, sizes),
            out_shape=[block_shape] * 2 + extra + [piece_shape] * (1 + len(alone)),
            in_specs=[hbm] * 2,
            out_specs=[vector] * (2 + len(bits) + 1 + len(alone)),
            scratch_shapes=[pltpu.SemaphoreType.DMA((2,))],
            compiler_params=pltpu.CompilerParams(vmem_limit_bytes=1 << 20),
            cost_estimate=pl.CostEstimate(flops=0, bytes_accessed=1 << 20, transcendentals=0),
            name="open",
        )(far(own), far(cache))
        own, cache = opened[:2]
        near = opened[2 + len(bits) :]
        first_hops = dict(zip(bits, opened[2 : 2 + len(bits)]))
        blocks = [cache] + gathered(first_hops, "seq", own.shape[0])
        diagonal = {mask: swapped(near[1 + at], "seq", mask) for at, mask in enumerate(alone)}
        pieces = [near[0]] + [diagonal.get(mask, blocks[mask]) for mask in range(1, half)]
        slot_shape = jax.ShapeDtypeStruct((page_count * piece, head_width), jnp.bfloat16)
        small = dict(
            out_shape=slot_shape,
            out_specs=vector,
            compiler_params=pltpu.CompilerParams(vmem_limit_bytes=2 << 20),
            cost_estimate=pl.CostEstimate(flops=0, bytes_accessed=4 << 20, transcendentals=0),
        )
        mine = pl.pallas_call(
            functools.partial(pick_kernel, sizes),
            in_specs=[scalars] + [vector] * len(pieces),
            name="pick",
            **small,
        )(table, *pieces)
        merged = pl.pallas_call(
            functools.partial(merge_kernel, sizes),
            in_specs=[scalars, vector, vector],
            name="merge",
            **small,
        )(table, mine, swapped(mine, "seq", half))
        pieces = [merged]
        for bit in bits[:-1]:
            sent = jnp.concatenate(pieces, 0) if bit > 1 else merged
            pieces.append(swapped(sent, "seq", bit))
    else:
        blocks, pieces = [], []
        for k in range(slash_count):
            distance = slash_shift[0, k]
            payload = jnp.where(own_shard < shards - distance, keys_values, cache_kv)
            blocks.append(rotate(payload, distance, shards).reshape(2 * row_count, head_width))
        whole = lax.all_gather(cache_kv, "seq", axis=0, tiled=True)
        for i in range(page_count):
            page = lax.dynamic_slice_in_dim(whole, vertical_pages[0, i] * PAGE, PAGE, 0)
            pieces.append(page.reshape(2 * PAGE, head_width))
    key_count = (1 + slash_count) * row_count + page_count * PAGE
    block = out_width // members
    send, keep = pl.pallas_call(
        functools.partial(attention_kernel, sizes),
        out_shape=[
            jax.ShapeDtypeStruct((members // 2, row_count, block), jnp.bfloat16),
            jax.ShapeDtypeStruct((members // 2, row_count, block), jnp.float32),
        ],
        in_specs=[scalars, vector, hbm] + [vector] * (1 + len(blocks) + len(pieces)),
        out_specs=[vector, vector],
        scratch_shapes=[
            pltpu.VMEM((2 * key_count, head_width), jnp.float32),
            pltpu.VMEM((key_count, head_width), jnp.bfloat16),
            pltpu.VMEM((key_count, head_width + LANES), jnp.bfloat16),
            pltpu.VMEM((2, row_count, key_count), jnp.float32),
            pltpu.VMEM((2, row_count, key_count), jnp.bfloat16),
            pltpu.VMEM((row_count, heads * head_width), jnp.bfloat16),
            pltpu.VMEM(out_proj.shape, out_proj.dtype),
            pltpu.SemaphoreType.DMA,
        ],
        compiler_params=pltpu.CompilerParams(vmem_limit_bytes=32 << 20),
        cost_estimate=pl.CostEstimate(
            flops=4 * heads * row_count * key_count * head_width
            + 2 * row_count * heads * head_width * out_width,
            bytes_accessed=8 << 20,
            transcendentals=heads * row_count * key_count,
        ),
        name="attend",
    )(table, queries, far(out_proj), own, *blocks, *pieces)
    step = 1
    while step < members:
        keep = keep + swapped(send, "head", step).astype(jnp.float32)
        step *= 2
        if step < members:
            send = keep[1::2].astype(jnp.bfloat16)
            keep = keep[0::2]
    return keep[0].astype(jnp.bfloat16)


def is_tree(shards):
    return 4 <= shards <= TREE_MAX and shards & (shards - 1) == 0


def solution(mesh):
    placed = (
        P("seq", "head"),
        P("seq", None, "head"),
        P("seq", None, "head"),
        P("head", None),
        P("head", None),
        P("seq", "head", None),
        P("head", None),
    )


    step = jax.shard_map(
        body, mesh=mesh, in_specs=placed, out_specs=P("seq", "head"), check_vma=False
    )
    if not is_tree(mesh.shape["seq"]):
        return step
    return step
```

```python
import functools
import math

import jax
import jax.numpy as jnp
from jax import lax
from jax.experimental import pallas as pl
from jax.experimental.pallas import tpu as pltpu
from jax.sharding import PartitionSpec as P


PAGE = 128
LANES = 128
FAR = 1e30
STRIP = 16
PARTS = 2
TREE_MAX = 16


def swapped(value, axis, mask):
    count = lax.axis_size(axis)
    return lax.ppermute(value, axis, [(source, source ^ mask) for source in range(count)])


def passed_along(value, axis, steps):
    count = lax.axis_size(axis)
    return lax.ppermute(value, axis, [(source, (source + steps) % count) for source in range(count)])


def gathered(first_hops, axis):
    blocks = {}
    for mask in range(1, lax.axis_size(axis)):
        low = mask & -mask
        source = blocks[mask - low] if mask > low else first_hops[low]
        blocks[mask] = swapped(source, axis, low)
    return [blocks[mask] for mask in range(1, len(blocks) + 1)]


def rotate(value, amount, shards):
    reduced = amount % shards
    for bit_number in range(max(1, (shards - 1).bit_length())):
        moved = passed_along(value, "seq", 1 << bit_number)
        value = jnp.where(reduced // (1 << bit_number) % 2 == 1, moved, value)
    return value


def decoded(sizes, table, me):
    shards, per_shard = sizes["shards"], sizes["per_shard"]
    slash_count, page_count = sizes["slash_count"], sizes["page_count"]
    slashes, pages = [], []
    for k in range(slash_count):
        distance = table[0, page_count + k]
        older = distance > me
        source = jnp.where(older, shards + me - distance, me - distance)
        slashes.append((source ^ me, older, table[0, page_count + slash_count + k] == 1))
    for i in range(page_count):
        owner = table[0, i] // per_shard
        clash = functools.reduce(
            jnp.logical_or,
            [live & older & (bits == (owner ^ me)) for bits, older, live in slashes],
        )
        pages.append((owner ^ me, table[0, i] - owner * per_shard, jnp.logical_not(clash)))
    return slashes, pages


def open_kernel(sizes, own_in, cache_in, own_near, cache_near, *rest):
    shards, per_shard, piece = sizes["shards"], sizes["per_shard"], sizes["piece"]
    sems, half = rest[-1], shards // 2
    hop_count = shards.bit_length() - 1
    hops, pieces = rest[:hop_count], rest[hop_count:-1]
    copies = [
        pltpu.make_async_copy(own_in, own_near, sems.at[0]),
        pltpu.make_async_copy(cache_in, cache_near, sems.at[1]),
    ]
    for copy in copies:
        copy.start()
    for copy in copies:
        copy.wait()
    me = lax.axis_index("seq")
    for number, hop in enumerate(hops):
        upper = (me >> number) & 1

        @pl.when(upper == 0)
        def _(hop=hop):
            hop[...] = own_near[...]

        @pl.when(upper == 1)
        def _(hop=hop):
            hop[...] = cache_near[...]

    for mask, place in enumerate(pieces):
        for at in range(per_shard):
            first = (at * half + mask) * piece
            place[pl.ds(at * piece, piece), :] = cache_near[pl.ds(first, piece), :]


def load_table(sources, table, lists, sems):
    copies = [
        pltpu.make_async_copy(source, place, sems.at[at])
        for at, (source, place) in enumerate(zip(sources, lists))
    ]
    for copy in copies:
        copy.start()
    for copy in copies:
        copy.wait()
    at = 0
    for part in lists:
        for entry in range(part.shape[1]):
            table[0, at] = part[0, entry]
            at += 1


def table_kernel(page_in, shift_in, live_in, table, *rest):
    load_table((page_in, shift_in, live_in), table, rest[:3], rest[3])


def stage_kernel(query_in, query_near, sem):
    copy = pltpu.make_async_copy(query_in, query_near, sem)
    copy.start()
    copy.wait()


def pick_kernel(sizes, page_in, shift_in, live_in, *rest):
    pieces, slots, table = rest[:-6], rest[-6], rest[-5]
    load_table((page_in, shift_in, live_in), table, rest[-4:-1], rest[-1])
    piece = sizes["piece"]
    _, pages = decoded(sizes, table, lax.axis_index("seq"))
    for i, (bits, place, _) in enumerate(pages):
        for mask, source in enumerate(pieces):

            @pl.when((bits & (len(pieces) - 1)) == mask)
            def _(source=source):
                first = pl.multiple_of(place * piece, piece)
                slots[pl.ds(i * piece, piece), :] = source[pl.ds(first, piece), :]


def merge_kernel(sizes, table, mine, other, merged):
    piece = sizes["piece"]
    _, pages = decoded(sizes, table, lax.axis_index("seq"))
    for i, (bits, _, _) in enumerate(pages):
        here = pl.ds(i * piece, piece)
        far = bits >= sizes["shards"] // 2

        @pl.when(far)
        def _(here=here):
            merged[here, :] = other[here, :]

        @pl.when(jnp.logical_not(far))
        def _(here=here):
            merged[here, :] = mine[here, :]


def first_kernel(sizes, table, query_ref, proj_ref, own_ref, *rest):
    shards, head_width = sizes["shards"], sizes["head_width"]
    slash_count, page_count = sizes["slash_count"], sizes["page_count"]
    page_rows, tree = sizes["page_rows"], sizes["tree"]
    piece = sizes["piece"]
    block_count = shards if tree else slash_count
    piece_count = shards // 2 if tree else page_count
    half = shards // 2
    blocks = rest[:block_count]
    pieces = rest[block_count : block_count + piece_count]
    rest = rest[block_count + piece_count :]
    send_ref, keep_ref, keys, values, proj, wide, scores, weights, attended, proj_sem = rest
    proj_copy = pltpu.make_async_copy(proj_ref, proj, proj_sem)
    proj_copy.start()
    rows = own_ref.shape[0] // 2
    slashes, pages = decoded(sizes, table, lax.axis_index("seq"))
    wide[pl.ds(0, 2 * rows), :] = own_ref[...].astype(jnp.float32)
    spans = [(0, rows, None)]
    first = rows
    for k, (bits, _, live) in enumerate(slashes):
        here = pl.ds(2 * first, 2 * rows)
        if tree:
            for mask in range(shards):

                @pl.when(bits == mask)
                def _(mask=mask):
                    wide[here, :] = blocks[mask][...].astype(jnp.float32)
        else:
            wide[here, :] = blocks[k][...].astype(jnp.float32)
        spans.append((first, rows, live))
        first += rows
    for i, (bits, _, is_open) in enumerate(pages):
        if tree:
            for mask in range(half):
                at = pl.multiple_of(2 * first + ((mask ^ bits) & (half - 1)) * piece, piece)
                source = pieces[mask][pl.ds(i * piece, piece), :]
                wide[pl.ds(at, piece), :] = source.astype(jnp.float32)
        else:
            wide[pl.ds(2 * first, 2 * page_rows), :] = pieces[i][...].astype(jnp.float32)
        spans.append((first, page_rows, is_open))
        first += page_rows
    keys[:, pl.ds(0, head_width)] = wide[pl.ds(0, first, stride=2), :].astype(jnp.bfloat16)
    values[:, pl.ds(0, head_width)] = wide[pl.ds(1, first, stride=2), :].astype(jnp.bfloat16)
    values[:, pl.ds(head_width, LANES)] = jnp.ones((first, LANES), jnp.bfloat16)
    for first, count, flag in spans:
        added = 0.0 if flag is None else jnp.where(flag, 0.0, -FAR)
        lanes = lax.broadcasted_iota(jnp.int32, (count, LANES), 1)
        keys[pl.ds(first, count), pl.ds(head_width, LANES)] = jnp.where(
            lanes == 0, added, 0.0
        ).astype(jnp.bfloat16)
    attend_rows(
        sizes, 0, query_ref, keys, values, scores, weights, attended
    )
    proj_copy.wait()
    project(sizes, attended, proj, send_ref, keep_ref)


def second_kernel(sizes, query_ref, keys, values, proj, send_ref, keep_ref, *scratch):
    scores, weights, attended = scratch
    attend_rows(sizes, 1, query_ref, keys, values, scores, weights, attended)
    project(sizes, attended, proj, send_ref, keep_ref)


def project(sizes, attended, proj, send_ref, keep_ref):
    members = sizes["members"]
    mine = lax.axis_index("head")
    block = proj.shape[1] // members
    for mask in range(members):
        column = pl.multiple_of((mine ^ mask) * block, block)
        term = jnp.dot(
            attended[...], proj[:, pl.ds(column, block)], preferred_element_type=jnp.float32
        )
        if mask % 2:
            send_ref[mask // 2] = term.astype(send_ref.dtype)
        else:
            keep_ref[mask // 2] = term


def attend_rows(sizes, part, query_ref, keys, values, scores, weights, attended):
    heads, head_width = sizes["heads"], sizes["head_width"]
    rows, part_rows, total_keys = query_ref.shape[0], attended.shape[0], keys.shape[0]
    group = rows // part_rows
    tile_count = heads // group
    one = (lax.broadcasted_iota(jnp.int32, (rows, LANES), 1) == 0).astype(jnp.bfloat16)
    scale = head_width**-0.5 * math.log2(math.e)
    starts = list(range(0, total_keys, rows))
    strips = list(range(0, rows, STRIP))

    def columns(tile, place):
        return pl.ds((tile * group + place) * head_width, head_width)

    def score(tile, start):
        query = jnp.concatenate(
            [query_ref[pl.ds(part * part_rows, part_rows), columns(tile, j)] for j in range(group)], 0
        )
        here = pl.ds(start, min(rows, total_keys - start))
        scores[tile % 2, :, here] = lax.dot_general(
            jnp.concatenate([query, one], 1),
            keys[here, :],
            (((1,), (1,)), ((), ())),
            preferred_element_type=jnp.float32,
        )

    def weigh(tile, top):
        here = pl.ds(top, STRIP)
        local = part * part_rows + top % part_rows
        diagonal = local // LANES
        row = lax.broadcasted_iota(jnp.int32, (STRIP, LANES), 0) + (local - diagonal * LANES)
        causal = row >= lax.broadcasted_iota(jnp.int32, (STRIP, LANES), 1)
        hidden = range((diagonal + 1) * LANES, rows, LANES)
        tiles = {}
        for at in range(0, total_keys, LANES):
            if at not in hidden:
                tiles[at] = scores[tile % 2, here, pl.ds(at, LANES)]
        tiles[diagonal * LANES] = jnp.where(causal, tiles[diagonal * LANES], -FAR)
        highest = jnp.max(functools.reduce(jnp.maximum, tiles.values()), axis=1, keepdims=True)
        for at, entry in tiles.items():
            weights[tile % 2, here, pl.ds(at, LANES)] = jnp.exp2((entry - highest) * scale).astype(
                jnp.bfloat16
            )
        for at in hidden:
            weights[tile % 2, here, pl.ds(at, LANES)] = jnp.zeros((STRIP, LANES), jnp.bfloat16)

    for start in starts:
        score(0, start)
    for tile in range(tile_count):
        for number, start in enumerate(starts):
            if tile + 1 < tile_count:
                score(tile + 1, start)
            low, high = (len(strips) * (number + more) // len(starts) for more in (0, 1))
            for top in strips[low:high]:
                weigh(tile, top)
        total = jnp.dot(weights[tile % 2], values[...], preferred_element_type=jnp.float32)
        mixed = (total[:, :head_width] / total[:, head_width:]).astype(jnp.bfloat16)
        for j in range(group):
            attended[:, columns(tile, j)] = mixed[j * part_rows : (j + 1) * part_rows]


def body(queries, keys_values, cache_kv, vertical_pages, slash_shift, slash_live, out_proj):
    row_count = queries.shape[0]
    head_width = keys_values.shape[2]
    heads = queries.shape[1] // head_width
    shards = lax.axis_size("seq")
    members = lax.axis_size("head")
    slash_count = slash_shift.shape[1]
    page_count = vertical_pages.shape[1]
    per_shard = row_count // PAGE
    out_width = out_proj.shape[1]
    own = keys_values.reshape(2 * row_count, head_width)
    cache = cache_kv.reshape(2 * row_count, head_width)
    tree = is_tree(shards)
    piece = 2 * PAGE // (shards // 2) if tree else 0
    sizes = dict(
        shards=shards, heads=heads, head_width=head_width, slash_count=slash_count,
        page_count=page_count, page_rows=PAGE, per_shard=per_shard, members=members, tree=tree,
        piece=piece,
    )
    scalars = pl.BlockSpec(memory_space=pltpu.SMEM)
    vector = pl.BlockSpec(memory_space=pltpu.VMEM)
    hbm = pl.BlockSpec(memory_space=pltpu.HBM)
    far = functools.partial(pltpu.with_memory_space_constraint, memory_space=pltpu.HBM)
    lists = [vertical_pages, slash_shift, slash_live.reshape(1, slash_count)]
    table_size = sum(part.shape[1] for part in lists)
    queries = pl.pallas_call(
        stage_kernel,
        out_shape=jax.ShapeDtypeStruct(queries.shape, queries.dtype),
        in_specs=[hbm],
        out_specs=vector,
        scratch_shapes=[pltpu.SemaphoreType.DMA],
        compiler_params=pltpu.CompilerParams(vmem_limit_bytes=1 << 20),
        cost_estimate=pl.CostEstimate(flops=0, bytes_accessed=2 << 20, transcendentals=0),
        name="stage",
    )(far(queries))
    table_shape = jax.ShapeDtypeStruct((1, table_size), jnp.int32)
    list_scratch = [pltpu.SMEM(part.shape, jnp.int32) for part in lists]
    list_scratch.append(pltpu.SemaphoreType.DMA((3,)))
    own_shard = lax.axis_index("seq")
    if tree:
        half = shards // 2
        bits = [1 << number for number in range(shards.bit_length() - 1)]
        block_shape = jax.ShapeDtypeStruct(own.shape, own.dtype)
        piece_rows = per_shard * piece
        piece_shape = jax.ShapeDtypeStruct((piece_rows, head_width), own.dtype)
        opened = pl.pallas_call(
            functools.partial(open_kernel, sizes),
            out_shape=[block_shape] * (2 + len(bits)) + [piece_shape] * half,
            in_specs=[hbm] * 2,
            out_specs=[vector] * (2 + len(bits) + half),
            scratch_shapes=[pltpu.SemaphoreType.DMA((2,))],
            compiler_params=pltpu.CompilerParams(vmem_limit_bytes=1 << 20),
            cost_estimate=pl.CostEstimate(flops=0, bytes_accessed=1 << 20, transcendentals=0),
            name="open",
        )(far(own), far(cache))
        own, cache = opened[:2]
        near = opened[2 + len(bits) :]
        first_hops = dict(zip(bits, opened[2 : 2 + len(bits)]))
        blocks = [cache] + gathered(first_hops, "seq")
        pieces = [near[0]] + [swapped(near[mask], "seq", mask) for mask in range(1, half)]
        slot_shape = jax.ShapeDtypeStruct((page_count * piece, head_width), jnp.bfloat16)
        small = dict(
            compiler_params=pltpu.CompilerParams(vmem_limit_bytes=2 << 20),
            cost_estimate=pl.CostEstimate(flops=0, bytes_accessed=4 << 20, transcendentals=0),
        )
        mine, table = pl.pallas_call(
            functools.partial(pick_kernel, sizes),
            out_shape=[slot_shape, table_shape],
            in_specs=[hbm] * 3 + [vector] * len(pieces),
            out_specs=[vector, scalars],
            scratch_shapes=list_scratch,
            name="pick",
            **small,
        )(*map(far, lists), *pieces)
        merged = pl.pallas_call(
            functools.partial(merge_kernel, sizes),
            out_shape=slot_shape,
            in_specs=[scalars, vector, vector],
            out_specs=vector,
            name="merge",
            **small,
        )(table, mine, swapped(mine, "seq", half))
        pieces = {0: merged}
        for mask in range(1, half):
            top = 1 << (mask.bit_length() - 1)
            pieces[mask] = swapped(pieces[mask - top], "seq", top)
        pieces = list(pieces.values())
    else:
        table = pl.pallas_call(
            table_kernel,
            out_shape=table_shape,
            in_specs=[hbm] * 3,
            out_specs=scalars,
            scratch_shapes=list_scratch,
            name="table",
        )(*map(far, lists))
        blocks, pieces = [], []
        for k in range(slash_count):
            distance = slash_shift[0, k]
            payload = jnp.where(own_shard < shards - distance, keys_values, cache_kv)
            blocks.append(rotate(payload, distance, shards).reshape(2 * row_count, head_width))
        whole = lax.all_gather(cache_kv, "seq", axis=0, tiled=True)
        for i in range(page_count):
            page = lax.dynamic_slice_in_dim(whole, vertical_pages[0, i] * PAGE, PAGE, 0)
            pieces.append(page.reshape(2 * PAGE, head_width))
    key_count = (1 + slash_count) * row_count + page_count * PAGE
    block = out_width // members
    part_rows = row_count // PARTS
    term_shapes = [
        jax.ShapeDtypeStruct((members // 2, part_rows, block), jnp.bfloat16),
        jax.ShapeDtypeStruct((members // 2, part_rows, block), jnp.float32),
    ]
    wide_shape = jax.ShapeDtypeStruct((key_count, head_width + LANES), jnp.bfloat16)
    scratch = [
        pltpu.VMEM((2, row_count, key_count), jnp.float32),
        pltpu.VMEM((2, row_count, key_count), jnp.bfloat16),
        pltpu.VMEM((part_rows, heads * head_width), jnp.bfloat16),
    ]
    settings = dict(
        compiler_params=pltpu.CompilerParams(vmem_limit_bytes=24 << 20),
        cost_estimate=pl.CostEstimate(
            flops=2 * heads * row_count * key_count * head_width
            + row_count * heads * head_width * out_width,
            bytes_accessed=8 << 20,
            transcendentals=heads * row_count * key_count // 2,
        ),
    )
    send, keep, keys, values, proj = pl.pallas_call(
        functools.partial(first_kernel, sizes),
        out_shape=term_shapes
        + [wide_shape] * 2
        + [jax.ShapeDtypeStruct(out_proj.shape, out_proj.dtype)],
        in_specs=[scalars, vector, hbm] + [vector] * (1 + len(blocks) + len(pieces)),
        out_specs=[vector] * 5,
        scratch_shapes=[pltpu.VMEM((2 * key_count, head_width), jnp.float32)]
        + scratch
        + [pltpu.SemaphoreType.DMA],
        name="first",
        **settings,
    )(table, queries, far(out_proj), own, *blocks, *pieces)
    terms = [(send, keep)]
    terms.append(
        pl.pallas_call(
            functools.partial(second_kernel, sizes),
            out_shape=term_shapes,
            in_specs=[vector] * 4,
            out_specs=[vector] * 2,
            scratch_shapes=scratch,
            name="second",
            **settings,
        )(queries, keys, values, proj)
    )
    parts = []
    for send, keep in terms:
        step = 1
        while step < members:
            keep = keep + swapped(send, "head", step).astype(jnp.float32)
            step *= 2
            if step < members:
                send = keep[1::2].astype(jnp.bfloat16)
                keep = keep[0::2]
        parts.append(keep[0].astype(jnp.bfloat16))
    return jnp.concatenate(parts, 0)


def is_tree(shards):
    return 4 <= shards <= TREE_MAX and shards & (shards - 1) == 0


def solution(mesh):
    placed = (
        P("seq", "head"),
        P("seq", None, "head"),
        P("seq", None, "head"),
        P("head", None),
        P("head", None),
        P("seq", "head", None),
        P("head", None),
    )


    step = jax.shard_map(
        body, mesh=mesh, in_specs=placed, out_specs=P("seq", "head"), check_vma=False
    )
    if not is_tree(mesh.shape["seq"]):
        return step
    return step
```

```python
import functools
import math

import jax
import jax.numpy as jnp
from jax import lax
from jax.experimental import pallas as pl
from jax.experimental.pallas import tpu as pltpu
from jax.sharding import PartitionSpec as P


PAGE = 128
LANES = 128
FAR = 1e30
STRIP = 16
PARTS = 2
TREE_MAX = 16


def swapped(value, axis, mask):
    count = lax.axis_size(axis)
    return lax.ppermute(value, axis, [(source, source ^ mask) for source in range(count)])


def passed_along(value, axis, steps):
    count = lax.axis_size(axis)
    return lax.ppermute(value, axis, [(source, (source + steps) % count) for source in range(count)])


def gathered(first_hops, axis):
    blocks = {}
    for mask in range(1, lax.axis_size(axis)):
        low = mask & -mask
        source = blocks[mask - low] if mask > low else first_hops[low]
        blocks[mask] = swapped(source, axis, low)
    return [blocks[mask] for mask in range(1, len(blocks) + 1)]


def rotate(value, amount, shards):
    reduced = amount % shards
    for bit_number in range(max(1, (shards - 1).bit_length())):
        moved = passed_along(value, "seq", 1 << bit_number)
        value = jnp.where(reduced // (1 << bit_number) % 2 == 1, moved, value)
    return value


def decoded(sizes, table, me):
    shards, per_shard = sizes["shards"], sizes["per_shard"]
    slash_count, page_count = sizes["slash_count"], sizes["page_count"]
    slashes, pages = [], []
    for k in range(slash_count):
        distance = table[0, page_count + k]
        older = distance > me
        source = jnp.where(older, shards + me - distance, me - distance)
        slashes.append((source ^ me, older, table[0, page_count + slash_count + k] == 1))
    for i in range(page_count):
        owner = table[0, i] // per_shard
        clash = functools.reduce(
            jnp.logical_or,
            [live & older & (bits == (owner ^ me)) for bits, older, live in slashes],
        )
        pages.append((owner ^ me, table[0, i] - owner * per_shard, jnp.logical_not(clash)))
    return slashes, pages


def open_kernel(sizes, own_in, cache_in, own_near, cache_near, *rest):
    shards, per_shard, piece = sizes["shards"], sizes["per_shard"], sizes["piece"]
    sems, half = rest[-1], shards // 2
    hop_count = shards.bit_length() - 1
    hops, pieces = rest[:hop_count], rest[hop_count:-1]
    copies = [
        pltpu.make_async_copy(own_in, own_near, sems.at[0]),
        pltpu.make_async_copy(cache_in, cache_near, sems.at[1]),
    ]
    for copy in copies:
        copy.start()
    for copy in copies:
        copy.wait()
    me = lax.axis_index("seq")
    for number, hop in enumerate(hops):
        upper = (me >> number) & 1

        @pl.when(upper == 0)
        def _(hop=hop):
            hop[...] = own_near[...]

        @pl.when(upper == 1)
        def _(hop=hop):
            hop[...] = cache_near[...]

    for mask, place in enumerate(pieces):
        for at in range(per_shard):
            first = (at * half + mask) * piece
            place[pl.ds(at * piece, piece), :] = cache_near[pl.ds(first, piece), :]


def load_table(sources, table, lists, sems):
    copies = [
        pltpu.make_async_copy(source, place, sems.at[at])
        for at, (source, place) in enumerate(zip(sources, lists))
    ]
    for copy in copies:
        copy.start()
    for copy in copies:
        copy.wait()
    at = 0
    for part in lists:
        for entry in range(part.shape[1]):
            table[0, at] = part[0, entry]
            at += 1


def table_kernel(page_in, shift_in, live_in, table, *rest):
    load_table((page_in, shift_in, live_in), table, rest[:3], rest[3])


def stage_kernel(query_in, query_near, sem):
    copy = pltpu.make_async_copy(query_in, query_near, sem)
    copy.start()
    copy.wait()


def pick_kernel(sizes, page_in, shift_in, live_in, *rest):
    pieces, slots, table = rest[:-6], rest[-6], rest[-5]
    load_table((page_in, shift_in, live_in), table, rest[-4:-1], rest[-1])
    piece = sizes["piece"]
    _, pages = decoded(sizes, table, lax.axis_index("seq"))
    for i, (bits, place, _) in enumerate(pages):
        for mask, source in enumerate(pieces):

            @pl.when((bits & (len(pieces) - 1)) == mask)
            def _(source=source):
                first = pl.multiple_of(place * piece, piece)
                slots[pl.ds(i * piece, piece), :] = source[pl.ds(first, piece), :]


def merge_kernel(sizes, table, mine, other, merged):
    piece = sizes["piece"]
    _, pages = decoded(sizes, table, lax.axis_index("seq"))
    for i, (bits, _, _) in enumerate(pages):
        here = pl.ds(i * piece, piece)
        far = bits >= sizes["shards"] // 2

        @pl.when(far)
        def _(here=here):
            merged[here, :] = other[here, :]

        @pl.when(jnp.logical_not(far))
        def _(here=here):
            merged[here, :] = mine[here, :]


def first_kernel(sizes, table, query_ref, proj_ref, own_ref, *rest):
    shards, head_width = sizes["shards"], sizes["head_width"]
    slash_count, page_count = sizes["slash_count"], sizes["page_count"]
    page_rows, tree = sizes["page_rows"], sizes["tree"]
    piece = sizes["piece"]
    block_count = shards if tree else slash_count
    piece_count = shards // 2 if tree else page_count
    half = shards // 2
    blocks = rest[:block_count]
    pieces = rest[block_count : block_count + piece_count]
    rest = rest[block_count + piece_count :]
    send_ref, keep_ref, keys, values, proj, wide, scores, weights, attended, proj_sem = rest
    proj_copy = pltpu.make_async_copy(proj_ref, proj, proj_sem)
    proj_copy.start()
    rows = own_ref.shape[0] // 2
    slashes, pages = decoded(sizes, table, lax.axis_index("seq"))
    wide[pl.ds(0, 2 * rows), :] = own_ref[...].astype(jnp.float32)
    spans = [(0, rows, None)]
    first = rows
    for k, (bits, _, live) in enumerate(slashes):
        here = pl.ds(2 * first, 2 * rows)
        if tree:
            for mask in range(shards):

                @pl.when(bits == mask)
                def _(mask=mask):
                    wide[here, :] = blocks[mask][...].astype(jnp.float32)
        else:
            wide[here, :] = blocks[k][...].astype(jnp.float32)
        spans.append((first, rows, live))
        first += rows
    for i, (bits, _, is_open) in enumerate(pages):
        if tree:
            for mask in range(half):
                at = pl.multiple_of(2 * first + ((mask ^ bits) & (half - 1)) * piece, piece)
                source = pieces[mask][pl.ds(i * piece, piece), :]
                wide[pl.ds(at, piece), :] = source.astype(jnp.float32)
        else:
            wide[pl.ds(2 * first, 2 * page_rows), :] = pieces[i][...].astype(jnp.float32)
        spans.append((first, page_rows, is_open))
        first += page_rows
    keys[:, pl.ds(0, head_width)] = wide[pl.ds(0, first, stride=2), :].astype(jnp.bfloat16)
    values[:, pl.ds(0, head_width)] = wide[pl.ds(1, first, stride=2), :].astype(jnp.bfloat16)
    values[:, pl.ds(head_width, LANES)] = jnp.ones((first, LANES), jnp.bfloat16)
    for first, count, flag in spans:
        added = 0.0 if flag is None else jnp.where(flag, 0.0, -FAR)
        lanes = lax.broadcasted_iota(jnp.int32, (count, LANES), 1)
        keys[pl.ds(first, count), pl.ds(head_width, LANES)] = jnp.where(
            lanes == 0, added, 0.0
        ).astype(jnp.bfloat16)
    attend_rows(
        sizes, 0, query_ref, keys, values, scores, weights, attended
    )
    proj_copy.wait()
    project(sizes, attended, proj, send_ref, keep_ref)


def second_kernel(sizes, query_ref, keys, values, proj, send_ref, keep_ref, *scratch):
    scores, weights, attended = scratch
    attend_rows(sizes, 1, query_ref, keys, values, scores, weights, attended)
    project(sizes, attended, proj, send_ref, keep_ref)


def project(sizes, attended, proj, send_ref, keep_ref):
    members = sizes["members"]
    mine = lax.axis_index("head")
    block = proj.shape[1] // members
    for mask in range(members):
        column = pl.multiple_of((mine ^ mask) * block, block)
        term = jnp.dot(
            attended[...], proj[:, pl.ds(column, block)], preferred_element_type=jnp.float32
        )
        if mask % 2:
            send_ref[mask // 2] = term.astype(send_ref.dtype)
        else:
            keep_ref[mask // 2] = term


def attend_rows(sizes, part, query_ref, keys, values, scores, weights, attended):
    heads, head_width = sizes["heads"], sizes["head_width"]
    rows, part_rows, total_keys = query_ref.shape[0], attended.shape[0], keys.shape[0]
    group = rows // part_rows
    tile_count = heads // group
    one = (lax.broadcasted_iota(jnp.int32, (rows, LANES), 1) == 0).astype(jnp.bfloat16)
    scale = head_width**-0.5 * math.log2(math.e)
    starts = list(range(0, total_keys, rows))
    strips = list(range(0, rows, STRIP))

    def columns(tile, place):
        return pl.ds((tile * group + place) * head_width, head_width)

    def score(tile, start):
        query = jnp.concatenate(
            [query_ref[pl.ds(part * part_rows, part_rows), columns(tile, j)] for j in range(group)], 0
        )
        here = pl.ds(start, min(rows, total_keys - start))
        scores[tile % 2, :, here] = lax.dot_general(
            jnp.concatenate([query, one], 1),
            keys[here, :],
            (((1,), (1,)), ((), ())),
            preferred_element_type=jnp.float32,
        )

    def weigh(tile, top):
        here = pl.ds(top, STRIP)
        local = part * part_rows + top % part_rows
        diagonal = local // LANES
        row = lax.broadcasted_iota(jnp.int32, (STRIP, LANES), 0) + (local - diagonal * LANES)
        causal = row >= lax.broadcasted_iota(jnp.int32, (STRIP, LANES), 1)
        hidden = range((diagonal + 1) * LANES, rows, LANES)
        tiles = {}
        for at in range(0, total_keys, LANES):
            if at not in hidden:
                tiles[at] = scores[tile % 2, here, pl.ds(at, LANES)]
        tiles[diagonal * LANES] = jnp.where(causal, tiles[diagonal * LANES], -FAR)
        highest = jnp.max(functools.reduce(jnp.maximum, tiles.values()), axis=1, keepdims=True)
        for at, entry in tiles.items():
            weights[tile % 2, here, pl.ds(at, LANES)] = jnp.exp2((entry - highest) * scale).astype(
                jnp.bfloat16
            )
        for at in hidden:
            weights[tile % 2, here, pl.ds(at, LANES)] = jnp.zeros((STRIP, LANES), jnp.bfloat16)

    for start in starts:
        score(0, start)
    for tile in range(tile_count):
        for number, start in enumerate(starts):
            if tile + 1 < tile_count:
                score(tile + 1, start)
            low, high = (len(strips) * (number + more) // len(starts) for more in (0, 1))
            for top in strips[low:high]:
                weigh(tile, top)
        total = jnp.dot(weights[tile % 2], values[...], preferred_element_type=jnp.float32)
        mixed = (total[:, :head_width] / total[:, head_width:]).astype(jnp.bfloat16)
        for j in range(group):
            attended[:, columns(tile, j)] = mixed[j * part_rows : (j + 1) * part_rows]


def body(queries, keys_values, cache_kv, vertical_pages, slash_shift, slash_live, out_proj):
    row_count = queries.shape[0]
    head_width = keys_values.shape[2]
    heads = queries.shape[1] // head_width
    shards = lax.axis_size("seq")
    members = lax.axis_size("head")
    slash_count = slash_shift.shape[1]
    page_count = vertical_pages.shape[1]
    per_shard = row_count // PAGE
    out_width = out_proj.shape[1]
    own = keys_values.reshape(2 * row_count, head_width)
    cache = cache_kv.reshape(2 * row_count, head_width)
    tree = is_tree(shards)
    piece = 2 * PAGE // (shards // 2) if tree else 0
    sizes = dict(
        shards=shards, heads=heads, head_width=head_width, slash_count=slash_count,
        page_count=page_count, page_rows=PAGE, per_shard=per_shard, members=members, tree=tree,
        piece=piece,
    )
    scalars = pl.BlockSpec(memory_space=pltpu.SMEM)
    vector = pl.BlockSpec(memory_space=pltpu.VMEM)
    hbm = pl.BlockSpec(memory_space=pltpu.HBM)
    far = functools.partial(pltpu.with_memory_space_constraint, memory_space=pltpu.HBM)
    lists = [vertical_pages, slash_shift, slash_live.reshape(1, slash_count)]
    table_size = sum(part.shape[1] for part in lists)
    queries = pl.pallas_call(
        stage_kernel,
        out_shape=jax.ShapeDtypeStruct(queries.shape, queries.dtype),
        in_specs=[hbm],
        out_specs=vector,
        scratch_shapes=[pltpu.SemaphoreType.DMA],
        compiler_params=pltpu.CompilerParams(vmem_limit_bytes=1 << 20),
        cost_estimate=pl.CostEstimate(flops=0, bytes_accessed=2 << 20, transcendentals=0),
        name="stage",
    )(far(queries))
    table_shape = jax.ShapeDtypeStruct((1, table_size), jnp.int32)
    list_scratch = [pltpu.SMEM(part.shape, jnp.int32) for part in lists]
    list_scratch.append(pltpu.SemaphoreType.DMA((3,)))
    own_shard = lax.axis_index("seq")
    if tree:
        half = shards // 2
        bits = [1 << number for number in range(shards.bit_length() - 1)]
        block_shape = jax.ShapeDtypeStruct(own.shape, own.dtype)
        piece_rows = per_shard * piece
        piece_shape = jax.ShapeDtypeStruct((piece_rows, head_width), own.dtype)
        opened = pl.pallas_call(
            functools.partial(open_kernel, sizes),
            out_shape=[block_shape] * (2 + len(bits)) + [piece_shape] * half,
            in_specs=[hbm] * 2,
            out_specs=[vector] * (2 + len(bits) + half),
            scratch_shapes=[pltpu.SemaphoreType.DMA((2,))],
            compiler_params=pltpu.CompilerParams(vmem_limit_bytes=1 << 20),
            cost_estimate=pl.CostEstimate(flops=0, bytes_accessed=1 << 20, transcendentals=0),
            name="open",
        )(far(own), far(cache))
        own, cache = opened[:2]
        near = opened[2 + len(bits) :]
        first_hops = dict(zip(bits, opened[2 : 2 + len(bits)]))
        blocks = [cache] + gathered(first_hops, "seq")
        pieces = [near[0]] + [swapped(near[mask], "seq", mask) for mask in range(1, half)]
        slot_shape = jax.ShapeDtypeStruct((page_count * piece, head_width), jnp.bfloat16)
        small = dict(
            compiler_params=pltpu.CompilerParams(vmem_limit_bytes=2 << 20),
            cost_estimate=pl.CostEstimate(flops=0, bytes_accessed=4 << 20, transcendentals=0),
        )
        mine, table = pl.pallas_call(
            functools.partial(pick_kernel, sizes),
            out_shape=[slot_shape, table_shape],
            in_specs=[hbm] * 3 + [vector] * len(pieces),
            out_specs=[vector, scalars],
            scratch_shapes=list_scratch,
            name="pick",
            **small,
        )(*map(far, lists), *pieces)
        merged = pl.pallas_call(
            functools.partial(merge_kernel, sizes),
            out_shape=slot_shape,
            in_specs=[scalars, vector, vector],
            out_specs=vector,
            name="merge",
            **small,
        )(table, mine, swapped(mine, "seq", half))
        pieces = [merged] + [swapped(merged, "seq", mask) for mask in range(1, half)]
    else:
        table = pl.pallas_call(
            table_kernel,
            out_shape=table_shape,
            in_specs=[hbm] * 3,
            out_specs=scalars,
            scratch_shapes=list_scratch,
            name="table",
        )(*map(far, lists))
        blocks, pieces = [], []
        for k in range(slash_count):
            distance = slash_shift[0, k]
            payload = jnp.where(own_shard < shards - distance, keys_values, cache_kv)
            blocks.append(rotate(payload, distance, shards).reshape(2 * row_count, head_width))
        whole = lax.all_gather(cache_kv, "seq", axis=0, tiled=True)
        for i in range(page_count):
            page = lax.dynamic_slice_in_dim(whole, vertical_pages[0, i] * PAGE, PAGE, 0)
            pieces.append(page.reshape(2 * PAGE, head_width))
    key_count = (1 + slash_count) * row_count + page_count * PAGE
    block = out_width // members
    part_rows = row_count // PARTS
    term_shapes = [
        jax.ShapeDtypeStruct((members // 2, part_rows, block), jnp.bfloat16),
        jax.ShapeDtypeStruct((members // 2, part_rows, block), jnp.float32),
    ]
    wide_shape = jax.ShapeDtypeStruct((key_count, head_width + LANES), jnp.bfloat16)
    scratch = [
        pltpu.VMEM((2, row_count, key_count), jnp.float32),
        pltpu.VMEM((2, row_count, key_count), jnp.bfloat16),
        pltpu.VMEM((part_rows, heads * head_width), jnp.bfloat16),
    ]
    settings = dict(
        compiler_params=pltpu.CompilerParams(vmem_limit_bytes=24 << 20),
        cost_estimate=pl.CostEstimate(
            flops=2 * heads * row_count * key_count * head_width
            + row_count * heads * head_width * out_width,
            bytes_accessed=8 << 20,
            transcendentals=heads * row_count * key_count // 2,
        ),
    )
    send, keep, keys, values, proj = pl.pallas_call(
        functools.partial(first_kernel, sizes),
        out_shape=term_shapes
        + [wide_shape] * 2
        + [jax.ShapeDtypeStruct(out_proj.shape, out_proj.dtype)],
        in_specs=[scalars, vector, hbm] + [vector] * (1 + len(blocks) + len(pieces)),
        out_specs=[vector] * 5,
        scratch_shapes=[pltpu.VMEM((2 * key_count, head_width), jnp.float32)]
        + scratch
        + [pltpu.SemaphoreType.DMA],
        name="first",
        **settings,
    )(table, queries, far(out_proj), own, *blocks, *pieces)
    terms = [(send, keep)]
    terms.append(
        pl.pallas_call(
            functools.partial(second_kernel, sizes),
            out_shape=term_shapes,
            in_specs=[vector] * 4,
            out_specs=[vector] * 2,
            scratch_shapes=scratch,
            name="second",
            **settings,
        )(queries, keys, values, proj)
    )
    parts = []
    for send, keep in terms:
        step = 1
        while step < members:
            keep = keep + swapped(send, "head", step).astype(jnp.float32)
            step *= 2
            if step < members:
                send = keep[1::2].astype(jnp.bfloat16)
                keep = keep[0::2]
        parts.append(keep[0].astype(jnp.bfloat16))
    return jnp.concatenate(parts, 0)


def is_tree(shards):
    return 4 <= shards <= TREE_MAX and shards & (shards - 1) == 0


def solution(mesh):
    placed = (
        P("seq", "head"),
        P("seq", None, "head"),
        P("seq", None, "head"),
        P("head", None),
        P("head", None),
        P("seq", "head", None),
        P("head", None),
    )


    step = jax.shard_map(
        body, mesh=mesh, in_specs=placed, out_specs=P("seq", "head"), check_vma=False
    )
    if not is_tree(mesh.shape["seq"]):
        return step
    return step
```

```python
import functools
import math

import jax
import jax.numpy as jnp
from jax import lax
from jax.experimental import pallas as pl
from jax.experimental.pallas import tpu as pltpu
from jax.sharding import PartitionSpec as P


PAGE = 128
LANES = 128
FAR = 1e30
STRIP = 16
PARTS = 2
TREE_MAX = 16


def swapped(value, axis, mask):
    count = lax.axis_size(axis)
    return lax.ppermute(value, axis, [(source, source ^ mask) for source in range(count)])


def passed_along(value, axis, steps):
    count = lax.axis_size(axis)
    return lax.ppermute(value, axis, [(source, (source + steps) % count) for source in range(count)])


def gathered(first_hops, axis):
    blocks = {}
    for mask in range(1, lax.axis_size(axis)):
        low = mask & -mask
        source = blocks[mask - low] if mask > low else first_hops[low]
        blocks[mask] = swapped(source, axis, low)
    return [blocks[mask] for mask in range(1, len(blocks) + 1)]


def rotate(value, amount, shards):
    reduced = amount % shards
    for bit_number in range(max(1, (shards - 1).bit_length())):
        moved = passed_along(value, "seq", 1 << bit_number)
        value = jnp.where(reduced // (1 << bit_number) % 2 == 1, moved, value)
    return value


def decoded(sizes, table, me):
    shards, per_shard = sizes["shards"], sizes["per_shard"]
    slash_count, page_count = sizes["slash_count"], sizes["page_count"]
    slashes, pages = [], []
    for k in range(slash_count):
        distance = table[0, page_count + k]
        older = distance > me
        source = jnp.where(older, shards + me - distance, me - distance)
        slashes.append((source ^ me, older, table[0, page_count + slash_count + k] == 1))
    for i in range(page_count):
        owner = table[0, i] // per_shard
        clash = functools.reduce(
            jnp.logical_or,
            [live & older & (bits == (owner ^ me)) for bits, older, live in slashes],
        )
        pages.append((owner ^ me, table[0, i] - owner * per_shard, jnp.logical_not(clash)))
    return slashes, pages


def open_kernel(sizes, own_in, cache_in, own_near, cache_near, *rest):
    shards, per_shard, piece = sizes["shards"], sizes["per_shard"], sizes["piece"]
    sems, half = rest[-1], shards // 2
    hop_count = shards.bit_length() - 1
    hops, pieces = rest[:hop_count], rest[hop_count:-1]
    copies = [
        pltpu.make_async_copy(own_in, own_near, sems.at[0]),
        pltpu.make_async_copy(cache_in, cache_near, sems.at[1]),
    ]
    for copy in copies:
        copy.start()
    for copy in copies:
        copy.wait()
    me = lax.axis_index("seq")
    for number, hop in enumerate(hops):
        upper = (me >> number) & 1

        @pl.when(upper == 0)
        def _(hop=hop):
            hop[...] = own_near[...]

        @pl.when(upper == 1)
        def _(hop=hop):
            hop[...] = cache_near[...]

    for mask, place in enumerate(pieces):
        for at in range(per_shard):
            first = (at * half + mask) * piece
            place[pl.ds(at * piece, piece), :] = cache_near[pl.ds(first, piece), :]


def load_table(sources, table, lists, sems):
    copies = [
        pltpu.make_async_copy(source, place, sems.at[at])
        for at, (source, place) in enumerate(zip(sources, lists))
    ]
    for copy in copies:
        copy.start()
    for copy in copies:
        copy.wait()
    at = 0
    for part in lists:
        for entry in range(part.shape[1]):
            table[0, at] = part[0, entry]
            at += 1


def table_kernel(page_in, shift_in, live_in, table, *rest):
    load_table((page_in, shift_in, live_in), table, rest[:3], rest[3])


def stage_kernel(query_in, query_near, sem):
    copy = pltpu.make_async_copy(query_in, query_near, sem)
    copy.start()
    copy.wait()


def pick_kernel(sizes, table, *rest):
    pieces, slots = rest[:-1], rest[-1]
    piece = sizes["piece"]
    _, pages = decoded(sizes, table, lax.axis_index("seq"))
    for i, (bits, place, _) in enumerate(pages):
        for mask, source in enumerate(pieces):

            @pl.when((bits & (len(pieces) - 1)) == mask)
            def _(source=source):
                first = pl.multiple_of(place * piece, piece)
                slots[pl.ds(i * piece, piece), :] = source[pl.ds(first, piece), :]


def merge_kernel(sizes, table, mine, other, merged):
    piece = sizes["piece"]
    _, pages = decoded(sizes, table, lax.axis_index("seq"))
    for i, (bits, _, _) in enumerate(pages):
        here = pl.ds(i * piece, piece)
        far = bits >= sizes["shards"] // 2

        @pl.when(far)
        def _(here=here):
            merged[here, :] = other[here, :]

        @pl.when(jnp.logical_not(far))
        def _(here=here):
            merged[here, :] = mine[here, :]


def first_kernel(sizes, table, query_ref, proj_ref, own_ref, *rest):
    shards, head_width = sizes["shards"], sizes["head_width"]
    slash_count, page_count = sizes["slash_count"], sizes["page_count"]
    page_rows, tree = sizes["page_rows"], sizes["tree"]
    piece = sizes["piece"]
    block_count = shards if tree else slash_count
    piece_count = shards // 2 if tree else page_count
    half = shards // 2
    blocks = rest[:block_count]
    pieces = rest[block_count : block_count + piece_count]
    rest = rest[block_count + piece_count :]
    send_ref, keep_ref, keys, values, proj, wide, scores, weights, attended, proj_sem = rest
    proj_copy = pltpu.make_async_copy(proj_ref, proj, proj_sem)
    proj_copy.start()
    rows = own_ref.shape[0] // 2
    slashes, pages = decoded(sizes, table, lax.axis_index("seq"))
    wide[pl.ds(0, 2 * rows), :] = own_ref[...].astype(jnp.float32)
    spans = [(0, rows, None)]
    first = rows
    for k, (bits, _, live) in enumerate(slashes):
        here = pl.ds(2 * first, 2 * rows)
        if tree:
            for mask in range(shards):

                @pl.when(bits == mask)
                def _(mask=mask):
                    wide[here, :] = blocks[mask][...].astype(jnp.float32)
        else:
            wide[here, :] = blocks[k][...].astype(jnp.float32)
        spans.append((first, rows, live))
        first += rows
    for i, (bits, _, is_open) in enumerate(pages):
        if tree:
            for mask in range(half):
                at = pl.multiple_of(2 * first + ((mask ^ bits) & (half - 1)) * piece, piece)
                source = pieces[mask][pl.ds(i * piece, piece), :]
                wide[pl.ds(at, piece), :] = source.astype(jnp.float32)
        else:
            wide[pl.ds(2 * first, 2 * page_rows), :] = pieces[i][...].astype(jnp.float32)
        spans.append((first, page_rows, is_open))
        first += page_rows
    keys[:, pl.ds(0, head_width)] = wide[pl.ds(0, first, stride=2), :].astype(jnp.bfloat16)
    values[:, pl.ds(0, head_width)] = wide[pl.ds(1, first, stride=2), :].astype(jnp.bfloat16)
    values[:, pl.ds(head_width, LANES)] = jnp.ones((first, LANES), jnp.bfloat16)
    for first, count, flag in spans:
        added = 0.0 if flag is None else jnp.where(flag, 0.0, -FAR)
        lanes = lax.broadcasted_iota(jnp.int32, (count, LANES), 1)
        keys[pl.ds(first, count), pl.ds(head_width, LANES)] = jnp.where(
            lanes == 0, added, 0.0
        ).astype(jnp.bfloat16)
    attend_rows(
        sizes, 0, query_ref, keys, values, scores, weights, attended
    )
    proj_copy.wait()
    project(sizes, attended, proj, send_ref, keep_ref)


def second_kernel(sizes, query_ref, keys, values, proj, send_ref, keep_ref, *scratch):
    scores, weights, attended = scratch
    attend_rows(sizes, 1, query_ref, keys, values, scores, weights, attended)
    project(sizes, attended, proj, send_ref, keep_ref)


def project(sizes, attended, proj, send_ref, keep_ref):
    members = sizes["members"]
    mine = lax.axis_index("head")
    block = proj.shape[1] // members
    for mask in range(members):
        column = pl.multiple_of((mine ^ mask) * block, block)
        term = jnp.dot(
            attended[...], proj[:, pl.ds(column, block)], preferred_element_type=jnp.float32
        )
        if mask % 2:
            send_ref[mask // 2] = term.astype(send_ref.dtype)
        else:
            keep_ref[mask // 2] = term


def attend_rows(sizes, part, query_ref, keys, values, scores, weights, attended):
    heads, head_width = sizes["heads"], sizes["head_width"]
    rows, part_rows, total_keys = query_ref.shape[0], attended.shape[0], keys.shape[0]
    group = rows // part_rows
    tile_count = heads // group
    one = (lax.broadcasted_iota(jnp.int32, (rows, LANES), 1) == 0).astype(jnp.bfloat16)
    scale = head_width**-0.5 * math.log2(math.e)
    starts = list(range(0, total_keys, rows))
    strips = list(range(0, rows, STRIP))

    def columns(tile, place):
        return pl.ds((tile * group + place) * head_width, head_width)

    def score(tile, start):
        query = jnp.concatenate(
            [query_ref[pl.ds(part * part_rows, part_rows), columns(tile, j)] for j in range(group)], 0
        )
        here = pl.ds(start, min(rows, total_keys - start))
        scores[tile % 2, :, here] = lax.dot_general(
            jnp.concatenate([query, one], 1),
            keys[here, :],
            (((1,), (1,)), ((), ())),
            preferred_element_type=jnp.float32,
        )

    def weigh(tile, top):
        here = pl.ds(top, STRIP)
        local = part * part_rows + top % part_rows
        diagonal = local // LANES
        row = lax.broadcasted_iota(jnp.int32, (STRIP, LANES), 0) + (local - diagonal * LANES)
        causal = row >= lax.broadcasted_iota(jnp.int32, (STRIP, LANES), 1)
        hidden = range((diagonal + 1) * LANES, rows, LANES)
        tiles = {}
        for at in range(0, total_keys, LANES):
            if at not in hidden:
                tiles[at] = scores[tile % 2, here, pl.ds(at, LANES)]
        tiles[diagonal * LANES] = jnp.where(causal, tiles[diagonal * LANES], -FAR)
        highest = jnp.max(functools.reduce(jnp.maximum, tiles.values()), axis=1, keepdims=True)
        for at, entry in tiles.items():
            weights[tile % 2, here, pl.ds(at, LANES)] = jnp.exp2((entry - highest) * scale).astype(
                jnp.bfloat16
            )
        for at in hidden:
            weights[tile % 2, here, pl.ds(at, LANES)] = jnp.zeros((STRIP, LANES), jnp.bfloat16)

    for start in starts:
        score(0, start)
    for tile in range(tile_count):
        for number, start in enumerate(starts):
            if tile + 1 < tile_count:
                score(tile + 1, start)
            low, high = (len(strips) * (number + more) // len(starts) for more in (0, 1))
            for top in strips[low:high]:
                weigh(tile, top)
        total = jnp.dot(weights[tile % 2], values[...], preferred_element_type=jnp.float32)
        mixed = (total[:, :head_width] / total[:, head_width:]).astype(jnp.bfloat16)
        for j in range(group):
            attended[:, columns(tile, j)] = mixed[j * part_rows : (j + 1) * part_rows]


def body(queries, keys_values, cache_kv, vertical_pages, slash_shift, slash_live, out_proj):
    row_count = queries.shape[0]
    head_width = keys_values.shape[2]
    heads = queries.shape[1] // head_width
    shards = lax.axis_size("seq")
    members = lax.axis_size("head")
    slash_count = slash_shift.shape[1]
    page_count = vertical_pages.shape[1]
    per_shard = row_count // PAGE
    out_width = out_proj.shape[1]
    own = keys_values.reshape(2 * row_count, head_width)
    cache = cache_kv.reshape(2 * row_count, head_width)
    tree = is_tree(shards)
    piece = 2 * PAGE // (shards // 2) if tree else 0
    sizes = dict(
        shards=shards, heads=heads, head_width=head_width, slash_count=slash_count,
        page_count=page_count, page_rows=PAGE, per_shard=per_shard, members=members, tree=tree,
        piece=piece,
    )
    scalars = pl.BlockSpec(memory_space=pltpu.SMEM)
    vector = pl.BlockSpec(memory_space=pltpu.VMEM)
    hbm = pl.BlockSpec(memory_space=pltpu.HBM)
    far = functools.partial(pltpu.with_memory_space_constraint, memory_space=pltpu.HBM)
    lists = [vertical_pages, slash_shift, slash_live.reshape(1, slash_count)]
    table_size = sum(part.shape[1] for part in lists)
    queries = pl.pallas_call(
        stage_kernel,
        out_shape=jax.ShapeDtypeStruct(queries.shape, queries.dtype),
        in_specs=[hbm],
        out_specs=vector,
        scratch_shapes=[pltpu.SemaphoreType.DMA],
        compiler_params=pltpu.CompilerParams(vmem_limit_bytes=1 << 20),
        cost_estimate=pl.CostEstimate(flops=0, bytes_accessed=2 << 20, transcendentals=0),
        name="stage",
    )(far(queries))
    table_shape = jax.ShapeDtypeStruct((1, table_size), jnp.int32)
    list_scratch = [pltpu.SMEM(part.shape, jnp.int32) for part in lists]
    list_scratch.append(pltpu.SemaphoreType.DMA((3,)))
    table = pl.pallas_call(
        table_kernel,
        out_shape=table_shape,
        in_specs=[hbm] * 3,
        out_specs=scalars,
        scratch_shapes=list_scratch,
        compiler_params=pltpu.CompilerParams(vmem_limit_bytes=1 << 20),
        cost_estimate=pl.CostEstimate(flops=0, bytes_accessed=1 << 20, transcendentals=0),
        name="table",
    )(*map(far, lists))
    own_shard = lax.axis_index("seq")
    if tree:
        half = shards // 2
        bits = [1 << number for number in range(shards.bit_length() - 1)]
        block_shape = jax.ShapeDtypeStruct(own.shape, own.dtype)
        piece_rows = per_shard * piece
        piece_shape = jax.ShapeDtypeStruct((piece_rows, head_width), own.dtype)
        opened = pl.pallas_call(
            functools.partial(open_kernel, sizes),
            out_shape=[block_shape] * (2 + len(bits)) + [piece_shape] * half,
            in_specs=[hbm] * 2,
            out_specs=[vector] * (2 + len(bits) + half),
            scratch_shapes=[pltpu.SemaphoreType.DMA((2,))],
            compiler_params=pltpu.CompilerParams(vmem_limit_bytes=1 << 20),
            cost_estimate=pl.CostEstimate(flops=0, bytes_accessed=1 << 20, transcendentals=0),
            name="open",
        )(far(own), far(cache))
        own, cache = opened[:2]
        near = opened[2 + len(bits) :]
        first_hops = dict(zip(bits, opened[2 : 2 + len(bits)]))
        blocks = [cache] + gathered(first_hops, "seq")
        pieces = [near[0]] + [swapped(near[mask], "seq", mask) for mask in range(1, half)]
        slot_shape = jax.ShapeDtypeStruct((page_count * piece, head_width), jnp.bfloat16)
        small = dict(
            compiler_params=pltpu.CompilerParams(vmem_limit_bytes=2 << 20),
            cost_estimate=pl.CostEstimate(flops=0, bytes_accessed=4 << 20, transcendentals=0),
        )
        mine = pl.pallas_call(
            functools.partial(pick_kernel, sizes),
            out_shape=slot_shape,
            in_specs=[scalars] + [vector] * len(pieces),
            out_specs=vector,
            name="pick",
            **small,
        )(table, *pieces)
        merged = pl.pallas_call(
            functools.partial(merge_kernel, sizes),
            out_shape=slot_shape,
            in_specs=[scalars, vector, vector],
            out_specs=vector,
            name="merge",
            **small,
        )(table, mine, swapped(mine, "seq", half))
        pieces = [merged] + [swapped(merged, "seq", mask) for mask in range(1, half)]
    else:
        blocks, pieces = [], []
        for k in range(slash_count):
            distance = slash_shift[0, k]
            payload = jnp.where(own_shard < shards - distance, keys_values, cache_kv)
            blocks.append(rotate(payload, distance, shards).reshape(2 * row_count, head_width))
        whole = lax.all_gather(cache_kv, "seq", axis=0, tiled=True)
        for i in range(page_count):
            page = lax.dynamic_slice_in_dim(whole, vertical_pages[0, i] * PAGE, PAGE, 0)
            pieces.append(page.reshape(2 * PAGE, head_width))
    key_count = (1 + slash_count) * row_count + page_count * PAGE
    block = out_width // members
    part_rows = row_count // PARTS
    term_shapes = [
        jax.ShapeDtypeStruct((members // 2, part_rows, block), jnp.bfloat16),
        jax.ShapeDtypeStruct((members // 2, part_rows, block), jnp.float32),
    ]
    wide_shape = jax.ShapeDtypeStruct((key_count, head_width + LANES), jnp.bfloat16)
    scratch = [
        pltpu.VMEM((2, row_count, key_count), jnp.float32),
        pltpu.VMEM((2, row_count, key_count), jnp.bfloat16),
        pltpu.VMEM((part_rows, heads * head_width), jnp.bfloat16),
    ]
    settings = dict(
        compiler_params=pltpu.CompilerParams(vmem_limit_bytes=24 << 20),
        cost_estimate=pl.CostEstimate(
            flops=2 * heads * row_count * key_count * head_width
            + row_count * heads * head_width * out_width,
            bytes_accessed=8 << 20,
            transcendentals=heads * row_count * key_count // 2,
        ),
    )
    send, keep, keys, values, proj = pl.pallas_call(
        functools.partial(first_kernel, sizes),
        out_shape=term_shapes
        + [wide_shape] * 2
        + [jax.ShapeDtypeStruct(out_proj.shape, out_proj.dtype)],
        in_specs=[scalars, vector, hbm] + [vector] * (1 + len(blocks) + len(pieces)),
        out_specs=[vector] * 5,
        scratch_shapes=[pltpu.VMEM((2 * key_count, head_width), jnp.float32)]
        + scratch
        + [pltpu.SemaphoreType.DMA],
        name="first",
        **settings,
    )(table, queries, far(out_proj), own, *blocks, *pieces)
    terms = [(send, keep)]
    terms.append(
        pl.pallas_call(
            functools.partial(second_kernel, sizes),
            out_shape=term_shapes,
            in_specs=[vector] * 4,
            out_specs=[vector] * 2,
            scratch_shapes=scratch,
            name="second",
            **settings,
        )(queries, keys, values, proj)
    )
    parts = []
    for send, keep in terms:
        step = 1
        while step < members:
            keep = keep + swapped(send, "head", step).astype(jnp.float32)
            step *= 2
            if step < members:
                send = keep[1::2].astype(jnp.bfloat16)
                keep = keep[0::2]
        parts.append(keep[0].astype(jnp.bfloat16))
    return jnp.concatenate(parts, 0)


def is_tree(shards):
    return 4 <= shards <= TREE_MAX and shards & (shards - 1) == 0


def solution(mesh):
    placed = (
        P("seq", "head"),
        P("seq", None, "head"),
        P("seq", None, "head"),
        P("head", None),
        P("head", None),
        P("seq", "head", None),
        P("head", None),
    )


    step = jax.shard_map(
        body, mesh=mesh, in_specs=placed, out_specs=P("seq", "head"), check_vma=False
    )
    if not is_tree(mesh.shape["seq"]):
        return step
    return step
```
